128 devices in a mesh: ctx: 16 (over x_lo, y, core), kvh: 8 (over x_hi, z).
Axes of the slice: x: 4 (x_hi: 2, x_lo: 2; x = x_hi * 2 + x_lo), y: 4, z: 4, core: 2. Of those that a mesh axis runs over, the one named last changes fastest.
Arguments:
- x_kv: bfloat16 [4096, 3072], P('ctx'), may hold values from -17 to 17, as said below
- w_kv: bfloat16 [3072, 2048], P(None, 'kvh'), may hold values from -0.0546875 to 0.0546875
- queries: bfloat16 [3, 6144, 3072], P(None, 'ctx', 'kvh'), may hold values from -6 to 6
- d_out: bfloat16 [3, 6144, 3072], P(None, 'ctx', 'kvh'), may hold values from -12 to 12
- lse: float32 [3, 6144, 24], P(None, 'ctx', 'kvh'), may hold values from 7 to 10
- delta: float32 [3, 6144, 24], P(None, 'ctx', 'kvh'), may hold values from -24 to 24
- offsets: int32 [16], P('ctx'), may hold values from 1 to 4095
- block_mask: int32 [48, 32], P('ctx'), may hold values 0 or 1
Outputs:
- d_queries: bfloat16 [3, 6144, 3072], P(None, 'ctx', 'kvh')
- d_x: bfloat16 [4096, 3072], P('ctx', 'kvh')
- d_w: float32 [3072, 2048], P('ctx', 'kvh')
The draws below stay inside these ranges and needn't reach their ends.
Inputs may be any that keep to these rules, and one draw needn't show every extreme that they name: `x_kv`: feature scales differ from column to column.
All inputs are finite; a program needn't handle non-finite values.
Results may differ from the reference program's by a relative error of at most 0.012.
Values may be sent and summed in bfloat16 or wider, within the bound.
No kernel may reach another device: no remote copies, remote signals or barrier semaphores. Data moves between devices by JAX's collectives and lax.ppermute only.
A program may use at most 64 MiB of HBM per device.

```python
import jax
import jax.numpy as jnp
from jax import lax

D = 3072
H = 24
KVH = 8
HD = 128
NL = 3
QBLK = 128
KBLK = 128
Q_DEV = 384
QUERIES = 6144
S_KV = 4096
GROUP = 3
CTX_SHARDS = 16


def draw_x_kv(key, part):
    first, second = jax.random.split(jax.random.fold_in(key, 71))
    ramp = jnp.arange(D, dtype=jnp.float32) / D
    jitter = jax.random.uniform(first, (D,), jnp.float32, 0.0, 0.25)
    base = jnp.clip(jax.random.normal(second, (S_KV, D), jnp.float32), -6.0, 6.0)
    scale = 10.0 ** (0.5 * ramp + jitter)
    return (base * scale[None, :] * 0.5).astype(jnp.bfloat16)


def place_ends(values, rng, low, top_value):
    dims = values.shape
    place = [jax.random.randint(jax.random.fold_in(rng, axis), (), 0, dims[axis]) for axis in range(len(dims))]
    values = values.at[tuple(place)].set(low)
    longest = dims.index(max(dims))
    place[longest] = (place[longest] + 1) % dims[longest]
    return values.at[tuple(place)].set(top_value)


def shard_levels(stream_key, dims, shards, least, top_value):
    def one(axis_at, parts):
        heights = jax.random.uniform(jax.random.fold_in(jax.random.fold_in(stream_key, 6), axis_at), (parts,), jnp.float32, least / len(shards), top_value / len(shards))
        return jnp.repeat(jnp.exp(heights), dims[axis_at] // parts).reshape((-1,) + (1,) * (len(dims) - axis_at - 1))

    level = one(*shards[0])
    for cut in shards[1:]:
        level = level * one(*cut)
    return level


def bell_draw(own_key, dims, spread, reach, pieces=(), kind=jnp.bfloat16):
    entries = jax.random.normal(own_key, dims, jnp.float32) * spread
    if len(pieces) > 0:
        entries = shard_levels(own_key, dims, pieces, -0.22, 0.18) * entries
    return jnp.clip(entries, min=-reach, max=reach).astype(kind)


def setup_inputs(seed: int = 0) -> dict:
    key_of = jax.random.split(jax.random.key(seed), 9)
    return {
        "x_kv": draw_x_kv(jax.random.fold_in(key_of[8], 71), 0),
        "w_kv": bell_draw(key_of[1], (D, KVH * 2 * HD), (4 * D) ** -0.5, 0.0546875, ((1, 8),)),
        "queries": bell_draw(key_of[2], (NL, QUERIES, H * HD), 1.0, 6.0, ((1, 16), (2, 8))),
        "d_out": bell_draw(key_of[3], (NL, QUERIES, H * HD), 2.0, 12.0, ((1, 16), (2, 8))),
        "lse": jnp.clip(7.0 + 3.0 * jax.random.uniform(key_of[4], (NL, QUERIES, H), jnp.float32) ** shard_levels(key_of[4], (NL, QUERIES, H), ((1, 16), (2, 8)), -0.2, 0.2), 7.0, 10.0),
        "delta": bell_draw(key_of[5], (NL, QUERIES, H), 4.0, 24.0, ((1, 16), (2, 8)), jnp.float32),
        "offsets": place_ends(jax.random.randint(key_of[6], (CTX_SHARDS,), 1, S_KV), jax.random.fold_in(key_of[6], 1), 1, S_KV - 1).astype(jnp.int32),
        "block_mask": place_ends((jax.random.randint(key_of[7], (QUERIES // QBLK, S_KV // KBLK), 0, 4) < 3).astype(jnp.int32), jax.random.fold_in(key_of[7], 1), 0, 1),
    }


def reference(x_kv, w_kv, queries, d_out, lse, delta, offsets, block_mask):
    kv = jnp.dot(x_kv, w_kv, preferred_element_type=jnp.float32).astype(jnp.bfloat16)
    key_value_four = kv.astype(jnp.float32).reshape(S_KV, KVH, 2, HD)
    kmat = key_value_four[:, :, 0, :]
    value_matrix = key_value_four[:, :, 1, :]
    nblocks = QUERIES // QBLK
    keys = jnp.arange(S_KV, dtype=jnp.int32)
    scale = HD ** (-0.5)
    q_blocks = jnp.transpose(queries.reshape(NL, nblocks, QBLK, KVH, GROUP, HD), (1, 0, 2, 3, 4, 5))
    o_blocks = jnp.transpose(d_out.reshape(NL, nblocks, QBLK, KVH, GROUP, HD), (1, 0, 2, 3, 4, 5))
    lse_blocks = jnp.transpose(lse.reshape(NL, nblocks, QBLK, KVH, GROUP), (1, 0, 3, 4, 2))
    delta_blocks = jnp.transpose(delta.reshape(NL, nblocks, QBLK, KVH, GROUP), (1, 0, 3, 4, 2))
    block_ids = jnp.arange(nblocks, dtype=jnp.int32)

    def step_block(carry, inputs):
        dk_sum, dv_sum = carry
        q_block, o_block, lse_block, delta_block, index = inputs
        rows = index * QBLK + jnp.arange(QBLK, dtype=jnp.int32)
        limit = offsets[rows // Q_DEV] + rows % Q_DEV
        allowed = block_mask[index][keys // KBLK]
        visible = (allowed == 1)[None, :] & (keys[None, :] < limit[:, None])
        dq_layers = []
        for layer_index in range(NL):
            qmat = q_block[layer_index].astype(jnp.float32)
            output_matrix = o_block[layer_index].astype(jnp.float32)
            scores = jnp.einsum('qkgd,nkd->kgqn', qmat, kmat) * scale
            probs = jnp.where(visible[None, None], jnp.exp(scores - lse_block[layer_index][..., None]), jnp.float32(0.0))
            p_half = probs.astype(jnp.bfloat16).astype(jnp.float32)
            probability_gradient = jnp.einsum('qkgd,nkd->kgqn', output_matrix, value_matrix)
            dscore = (probs * (probability_gradient - delta_block[layer_index][..., None])).astype(jnp.bfloat16).astype(jnp.float32)
            dv_sum = dv_sum + jnp.einsum('kgqn,qkgd->nkd', p_half, output_matrix)
            dk_sum = dk_sum + jnp.einsum('kgqn,qkgd->nkd', dscore, qmat) * scale
            dq_layers.append((jnp.einsum('kgqn,nkd->qkgd', dscore, kmat) * scale).astype(jnp.bfloat16))
        return ((dk_sum, dv_sum), jnp.stack(dq_layers, axis=0))
    init = (jnp.zeros((S_KV, KVH, HD), jnp.float32), jnp.zeros((S_KV, KVH, HD), jnp.float32))
    (dk_sum, dv_sum), dq_all = lax.scan(step_block, init, (q_blocks, o_blocks, lse_blocks, delta_blocks, block_ids))
    d_queries = jnp.transpose(dq_all, (1, 0, 2, 3, 4, 5)).reshape(NL, QUERIES, H * HD)
    dkv = jnp.stack([dk_sum, dv_sum], axis=2).reshape(S_KV, KVH * 2 * HD)
    dkv_half = dkv.astype(jnp.bfloat16)
    d_x = jnp.dot(dkv_half, w_kv.T, preferred_element_type=jnp.float32).astype(jnp.bfloat16)
    grad = jnp.dot(x_kv.T, dkv_half, preferred_element_type=jnp.float32)
    msq = jnp.mean(grad * grad)
    d_w = grad / jnp.sqrt(msq + 1e-06)
    return (d_queries, d_x, d_w)
```

```python
import functools

import jax
import jax.numpy as jnp
from jax import lax
from jax.experimental import pallas as pl
from jax.experimental.pallas import tpu as pltpu
from jax.sharding import Mesh, PartitionSpec as P

D = 3072
KVH = 8
HD = 128
NL = 3
NLH = 9
KB = 16
QB = 6
LOG2E = 1.4426950408889634
C1 = LOG2E * HD ** (-0.5)
NEG = -1e30
NT = (((1,), (1,)), ((), ()))
NN = (((1,), (0,)), ((), ()))
TN = (((0,), (0,)), ((), ()))
C8 = ("xl", "y")
K8 = ("xh", "z")
ALL = ("xl", "y", "co", "xh", "z")

def attn_kernel(groups, ints_o, ints_p, co_ref, small_o, small_p, kv_ref, qo, qp, oo, op, dkv_ref, dqo_ref, dqp_ref,
                q_s, o_s, kT_s, acc_s, dq_s, p_s, ds_s, bias_s, lst, cnt, sem):
    f32=jnp.float32; bf=jnp.bfloat16
    copies=[pltpu.make_async_copy(a, d, sem.at[i]) for i,(a,d) in enumerate(
        [(qo,q_s.at[0]),(oo,o_s.at[0]),(qp,q_s.at[1]),(op,o_s.at[1])])]
    for c in copies: c.start()
    co=co_ref[0]
    acc_s[...]=jnp.zeros(acc_s.shape,f32)
    for kb in range(KB):
        kT_s[kb]=kv_ref[kb,:,:HD].T
    for s,ints in ((0,ints_o),(1,ints_p)):
        off=ints[96]
        for b in range(3):
            n=jnp.int32(0)
            for kb in range(KB):
                j,c=divmod(kb,2)
                i=(j//4)*8+(j%4)*2+co
                st=i*256+c*128
                vis=(ints[b*32+2*i+c]==1)&(st<off+(b*128+127))
                lst[s*3+b,n]=jnp.int32(kb)
                n=n+vis.astype(jnp.int32)
            cnt[s*3+b]=n
            lst[s*3+b,n]=jnp.int32(KB)
    for c in copies: c.wait()

    rowi=lax.broadcasted_iota(jnp.int32,(HD,HD),0)
    coli=lax.broadcasted_iota(jnp.int32,(HD,HD),1)
    dif=coli-rowi

    def qb_body(qb,_):
        s=qb//3; b=qb-3*s
        rows=pl.ds(pl.multiple_of(b*128,128),128)
        n=cnt[qb]
        off=jnp.where(s==0,ints_o[96],ints_p[96])+b*128
        dq_s[...]=jnp.zeros(dq_s.shape,f32)
        def qg(ref,lhs):
            return jnp.concatenate([ref[s,lh//3,rows,(lh%3)*HD:(lh%3+1)*HD] for lh in lhs],axis=0)
        def pair(t,_):
            kb0=lst[qb,2*t]
            kb1r=lst[qb,2*t+1]
            one=2*t+1>=n
            kb1=jnp.where(one,kb0,kb1r)
            def start(kb):
                j=kb//2
                return ((j//4)*8+(j%4)*2+co)*256+(kb-2*j)*128
            st0=start(kb0)
            st1=jnp.where(one,jnp.int32(1<<20),start(kb1))
            bias_s[0:HD]=jnp.where(dif>st0-off,f32(0),f32(NEG))
            bias_s[HD:]=jnp.where(dif>st1-off,f32(0),f32(NEG))
            K2=jnp.concatenate([kv_ref[kb0,:,:HD],kv_ref[kb1,:,:HD]],axis=0)
            V2=jnp.concatenate([kv_ref[kb0,:,HD:],kv_ref[kb1,:,HD:]],axis=0)
            K2T=jnp.concatenate([kT_s[kb0],kT_s[kb1]],axis=1)
            bias=bias_s[...]
            for g in groups:
                Q=qg(q_s,g); O=qg(o_s,g)
                ST=lax.dot_general(K2,Q,NT,preferred_element_type=f32)
                DP=lax.dot_general(V2,O,NT,preferred_element_type=f32)
                for u,lh in enumerate(g):
                    cs=slice(u*HD,(u+1)*HD)
                    lse=jnp.where(s==0,small_o[b,lh],small_p[b,lh])[None,:]*f32(LOG2E)
                    dl=jnp.where(s==0,small_o[b,9+lh],small_p[b,9+lh])[None,:]
                    p=jnp.exp2(ST[:,cs]*f32(C1)-lse+bias)
                    p_s[:,lh*HD:(lh+1)*HD]=p.astype(bf)
                    ds_s[:,lh*HD:(lh+1)*HD]=(p*(DP[:,cs]-dl)).astype(bf)
            allq=tuple(range(NLH))
            dv=lax.dot_general(p_s[...],qg(o_s,allq),NN,preferred_element_type=f32)
            dk=lax.dot_general(ds_s[...],qg(q_s,allq),NN,preferred_element_type=f32)
            acc_s[kb0,:,:HD]+=dk[:HD]
            acc_s[kb0,:,HD:]+=dv[:HD]
            acc_s[kb1,:,:HD]+=dk[HD:]
            acc_s[kb1,:,HD:]+=dv[HD:]
            dq_s[...]+=lax.dot_general(K2T,ds_s[...],NN,preferred_element_type=f32)
            return 0
        lax.fori_loop(0,(n+1)//2,pair,0)
        sc=f32(HD**(-0.5))
        @pl.when(s==0)
        def _(): dqo_ref[b]=dq_s[...]*sc
        @pl.when(s==1)
        def _(): dqp_ref[b]=(dq_s[...]*sc).astype(bf)
        return 0
    lax.fori_loop(0,QB,qb_body,0)
    sc=f32(HD**(-0.5))
    dkv_ref[:,:,:HD]=(acc_s[:,:,:HD]*sc).astype(bf)
    dkv_ref[:,:,HD:]=acc_s[:,:,HD:].astype(bf)

def attn(ints_o,ints_p,co,small_o,small_p,kv,qo,qp,oo,op,groups=((0,1),(2,3),(4,5),(6,7),(8,))):
    f32=jnp.float32; bf=jnp.bfloat16
    S=pl.BlockSpec(memory_space=pltpu.SMEM); V=pl.BlockSpec(memory_space=pltpu.VMEM); A=pl.BlockSpec(memory_space=pl.ANY)
    return pl.pallas_call(
        functools.partial(attn_kernel,groups),
        out_shape=(jax.ShapeDtypeStruct((KB,HD,2*HD),bf),jax.ShapeDtypeStruct((3,HD,NLH*HD),f32),jax.ShapeDtypeStruct((3,HD,NLH*HD),bf)),
        in_specs=[S,S,S,V,V,V,A,A,A,A], out_specs=(V,V,V),
        scratch_shapes=[pltpu.VMEM((2,NL,384,384),bf),pltpu.VMEM((2,NL,384,384),bf),pltpu.VMEM((KB,HD,HD),bf),
            pltpu.VMEM((KB,HD,2*HD),f32),pltpu.VMEM((HD,NLH*HD),f32),pltpu.VMEM((2*HD,NLH*HD),bf),pltpu.VMEM((2*HD,NLH*HD),bf),
            pltpu.VMEM((2*HD,HD),f32),pltpu.SMEM((QB,KB+1),jnp.int32),pltpu.SMEM((QB,),jnp.int32),pltpu.SemaphoreType.DMA((4,))],
        name="attn",
    )(ints_o,ints_p,co,small_o,small_p,kv,qo,qp,oo,op)


def dx_kernel(g_ref, w_ref, out_ref):
    acc = lax.dot_general(g_ref[0], w_ref[0], NT, preferred_element_type=jnp.float32)
    for k in range(1, 8):
        acc += lax.dot_general(g_ref[k], w_ref[k], NT, preferred_element_type=jnp.float32)
    out_ref[...] = acc.astype(jnp.bfloat16)


def dq_kernel(a_ref, b_ref, out_ref):
    for b in range(3):
        for lh in range(NLH):
            cs = slice(lh * HD, (lh + 1) * HD)
            t = a_ref[b, :, cs] + b_ref[b, :, cs].astype(jnp.float32)
            h = lh % 3
            out_ref[lh // 3, b * HD : (b + 1) * HD, h * HD : (h + 1) * HD] = t.T.astype(jnp.bfloat16)


def swap(a):
    return lax.ppermute(a, "co", [(0, 1), (1, 0)])


def body(x_kv, w_kv, queries, d_out, lse, delta, offsets, block_mask):
    f32 = jnp.float32
    bf = jnp.bfloat16
    co = lax.axis_index("co")
    kv_local = jnp.dot(x_kv, w_kv, preferred_element_type=f32).astype(bf)
    kv_all = lax.all_to_all(jnp.broadcast_to(kv_local[None], (8, 256, 256)), C8, 0, 0)
    ints = jnp.concatenate([block_mask.reshape(96), offsets, jnp.zeros((31,), jnp.int32)])
    rows = jnp.concatenate([lse, delta], axis=2).reshape(NL, 3, HD, 2, 3)
    small = jnp.transpose(rows, (1, 3, 0, 4, 2)).reshape(3, 2 * NLH, HD)
    w_all = lax.all_to_all(w_kv.reshape(8, 384, 256), K8, 0, 0)
    dkv, dqo, dqp = attn(
        ints, swap(ints), co.reshape(1).astype(jnp.int32), small, swap(small),
        kv_all.reshape(KB, HD, 2 * HD), queries, swap(queries), d_out, swap(d_out),
    )
    dkv_r = lax.all_to_all(dkv.reshape(8, 256, 256), C8, 0, 0)
    dkv_half = jnp.sum(dkv_r.astype(f32), axis=0).astype(bf)
    dw_part = lax.dot_general(x_kv, dkv_half, TN, preferred_element_type=f32).astype(bf)
    dw_part = dw_part.reshape(8, 2, 192, 256)
    mine = lax.dynamic_index_in_dim(dw_part, co, 1, False)
    other = swap(lax.dynamic_index_in_dim(dw_part, 1 - co, 1, False))
    chip = (mine.astype(f32) + other.astype(f32)).astype(bf)
    grad = jnp.sum(lax.all_to_all(chip, C8, 0, 0).astype(f32), axis=0)
    squares = jnp.sum(grad * grad)
    g_all = lax.all_to_all(jnp.broadcast_to(dkv_half[None], (8, 256, 256)), K8, 0, 0)
    parts = lax.all_to_all(jnp.broadcast_to(squares.reshape(1, 1, 1), (128, 8, 128)), ALL, 0, 0)
    total = jnp.sum(parts[:, 0, 0])
    d_w = grad / jnp.sqrt(total / (D * KVH * 2 * HD) + 1e-06)
    d_x = pl.pallas_call(
        dx_kernel, out_shape=jax.ShapeDtypeStruct((256, 384), bf), name="dx"
    )(g_all, w_all)
    d_queries = pl.pallas_call(
        dq_kernel, out_shape=jax.ShapeDtypeStruct((NL, 384, 384), bf), name="dqfin"
    )(dqo, swap(dqp))
    return (d_queries, d_x, d_w)


def solution(mesh):
    mesh5 = Mesh(mesh.devices.reshape(2, 4, 2, 2, 4), ALL)
    ctx = ("xl", "y", "co")
    kvh = ("xh", "z")
    in_specs = (
        P(ctx, None),
        P(None, kvh),
        P(None, ctx, kvh),
        P(None, ctx, kvh),
        P(None, ctx, kvh),
        P(None, ctx, kvh),
        P(ctx),
        P(ctx, None),
    )
    out_specs = (P(None, ctx, kvh), P(ctx, kvh), P(ctx, kvh))
    return jax.shard_map(body, mesh=mesh5, in_specs=in_specs, out_specs=out_specs, check_vma=False)
```

```python
import functools

import jax
import jax.numpy as jnp
from jax import lax
from jax.experimental import pallas as pl
from jax.experimental.pallas import tpu as pltpu
from jax.sharding import Mesh, PartitionSpec as P

D = 3072
KVH = 8
HD = 128
NL = 3
NLH = 9
KB = 16
QB = 6
LOG2E = 1.4426950408889634
C1 = LOG2E * HD ** (-0.5)
NEG = -1e30
NT = (((1,), (1,)), ((), ()))
NN = (((1,), (0,)), ((), ()))
C8 = ("xl", "y")
K8 = ("xh", "z")
ALL = ("xl", "y", "co", "xh", "z")


def attn_kernel(groups, ints_o, ints_p, co_ref, small_o, small_p, kv_ref, qo, qp, oo, op, dkv_ref, dqo_ref, dqp_ref,
                q_s, o_s, kT_s, acc_s, dq_s, p_s, ds_s, bias_s, lst, cnt, sem):
    f32=jnp.float32; bf=jnp.bfloat16
    copies=[pltpu.make_async_copy(a, d, sem.at[i]) for i,(a,d) in enumerate(
        [(qo,q_s.at[0]),(oo,o_s.at[0]),(qp,q_s.at[1]),(op,o_s.at[1])])]
    for c in copies: c.start()
    co=co_ref[0]
    acc_s[...]=jnp.zeros(acc_s.shape,f32)
    for kb in range(KB):
        kT_s[kb]=kv_ref[kb,:,:HD].T
    for s,ints in ((0,ints_o),(1,ints_p)):
        off=ints[96]
        for b in range(3):
            n=jnp.int32(0)
            for kb in range(KB):
                j,c=divmod(kb,2)
                i=(j//4)*8+(j%4)*2+co
                st=i*256+c*128
                vis=(ints[b*32+2*i+c]==1)&(st<off+(b*128+127))
                lst[s*3+b,n]=jnp.int32(kb)
                n=n+vis.astype(jnp.int32)
            cnt[s*3+b]=n
            lst[s*3+b,n]=jnp.int32(KB)
    for c in copies: c.wait()

    rowi=lax.broadcasted_iota(jnp.int32,(HD,HD),0)
    coli=lax.broadcasted_iota(jnp.int32,(HD,HD),1)
    dif=coli-rowi

    def qb_body(qb,_):
        s=qb//3; b=qb-3*s
        rows=pl.ds(pl.multiple_of(b*128,128),128)
        n=cnt[qb]
        off=jnp.where(s==0,ints_o[96],ints_p[96])+b*128
        dq_s[...]=jnp.zeros(dq_s.shape,f32)
        def qg(ref,lhs):
            return jnp.concatenate([ref[s,lh//3,rows,(lh%3)*HD:(lh%3+1)*HD] for lh in lhs],axis=0)
        def pair(t,_):
            kb0=lst[qb,2*t]
            kb1r=lst[qb,2*t+1]
            one=2*t+1>=n
            kb1=jnp.where(one,kb0,kb1r)
            def start(kb):
                j=kb//2
                return ((j//4)*8+(j%4)*2+co)*256+(kb-2*j)*128
            st0=start(kb0)
            st1=jnp.where(one,jnp.int32(1<<20),start(kb1))
            bias_s[0:HD]=jnp.where(dif>st0-off,f32(0),f32(NEG))
            bias_s[HD:]=jnp.where(dif>st1-off,f32(0),f32(NEG))
            K2=jnp.concatenate([kv_ref[kb0,:,:HD],kv_ref[kb1,:,:HD]],axis=0)
            V2=jnp.concatenate([kv_ref[kb0,:,HD:],kv_ref[kb1,:,HD:]],axis=0)
            K2T=jnp.concatenate([kT_s[kb0],kT_s[kb1]],axis=1)
            bias=bias_s[...]
            for g in groups:
                Q=qg(q_s,g); O=qg(o_s,g)
                ST=lax.dot_general(K2,Q,NT,preferred_element_type=f32)
                DP=lax.dot_general(V2,O,NT,preferred_element_type=f32)
                for u,lh in enumerate(g):
                    cs=slice(u*HD,(u+1)*HD)
                    lse=jnp.where(s==0,small_o[b,lh],small_p[b,lh])[None,:]*f32(LOG2E)
                    dl=jnp.where(s==0,small_o[b,9+lh],small_p[b,9+lh])[None,:]
                    p=jnp.exp2(ST[:,cs]*f32(C1)-lse+bias)
                    p_s[:,lh*HD:(lh+1)*HD]=p.astype(bf)
                    ds_s[:,lh*HD:(lh+1)*HD]=(p*(DP[:,cs]-dl)).astype(bf)
            allq=tuple(range(NLH))
            dv=lax.dot_general(p_s[...],qg(o_s,allq),NN,preferred_element_type=f32)
            dk=lax.dot_general(ds_s[...],qg(q_s,allq),NN,preferred_element_type=f32)
            acc_s[kb0,:,:HD]+=dk[:HD]
            acc_s[kb0,:,HD:]+=dv[:HD]
            acc_s[kb1,:,:HD]+=dk[HD:]
            acc_s[kb1,:,HD:]+=dv[HD:]
            dq_s[...]+=lax.dot_general(K2T,ds_s[...],NN,preferred_element_type=f32)
            return 0
        lax.fori_loop(0,(n+1)//2,pair,0)
        sc=f32(HD**(-0.5))
        @pl.when(s==0)
        def _(): dqo_ref[b]=dq_s[...]*sc
        @pl.when(s==1)
        def _(): dqp_ref[b]=(dq_s[...]*sc).astype(bf)
        return 0
    lax.fori_loop(0,QB,qb_body,0)
    sc=f32(HD**(-0.5))
    dkv_ref[:,:,:HD]=(acc_s[:,:,:HD]*sc).astype(bf)
    dkv_ref[:,:,HD:]=acc_s[:,:,HD:].astype(bf)


def attn(ints_o,ints_p,co,small_o,small_p,kv,qo,qp,oo,op,groups=((0,1),(2,3),(4,5),(6,7),(8,))):
    f32=jnp.float32; bf=jnp.bfloat16
    S=pl.BlockSpec(memory_space=pltpu.SMEM); V=pl.BlockSpec(memory_space=pltpu.VMEM); A=pl.BlockSpec(memory_space=pl.ANY)
    return pl.pallas_call(
        functools.partial(attn_kernel,groups),
        out_shape=(jax.ShapeDtypeStruct((KB,HD,2*HD),bf),jax.ShapeDtypeStruct((3,HD,NLH*HD),f32),jax.ShapeDtypeStruct((3,HD,NLH*HD),bf)),
        in_specs=[S,S,S,V,V,V,A,A,A,A], out_specs=(V,V,V),
        scratch_shapes=[pltpu.VMEM((2,NL,384,384),bf),pltpu.VMEM((2,NL,384,384),bf),pltpu.VMEM((KB,HD,HD),bf),
            pltpu.VMEM((KB,HD,2*HD),f32),pltpu.VMEM((HD,NLH*HD),f32),pltpu.VMEM((2*HD,NLH*HD),bf),pltpu.VMEM((2*HD,NLH*HD),bf),
            pltpu.VMEM((2*HD,HD),f32),pltpu.SMEM((QB,KB+1),jnp.int32),pltpu.SMEM((QB,),jnp.int32),pltpu.SemaphoreType.DMA((4,))],
        name="attn",
    )(ints_o,ints_p,co,small_o,small_p,kv,qo,qp,oo,op)


VM = pl.BlockSpec(memory_space=pltpu.VMEM)
SM = pl.BlockSpec(memory_space=pltpu.SMEM)


def sum_kernel(r_ref, out_ref):
    acc = r_ref[0].astype(jnp.float32)
    for k in range(1, 8):
        acc += r_ref[k].astype(jnp.float32)
    out_ref[...] = acc.astype(jnp.bfloat16)


def dw_kernel(xa_ref, xb_ref, ga_ref, gb_ref, out_ref):
    for k in range(8):
        acc = lax.dot_general(xa_ref[k], ga_ref[...], NN, preferred_element_type=jnp.float32)
        acc += lax.dot_general(xb_ref[k], gb_ref[...], NN, preferred_element_type=jnp.float32)
        out_ref[k] = acc.astype(jnp.bfloat16)


def grad_kernel(r_ref, grad_ref, sq_ref):
    acc = r_ref[0].astype(jnp.float32)
    for k in range(1, 8):
        acc += r_ref[k].astype(jnp.float32)
    grad_ref[...] = acc
    sq = jnp.sum(jnp.sum(acc * acc, axis=0, keepdims=True), axis=1, keepdims=True)
    sq_ref[...] = jnp.broadcast_to(sq, sq_ref.shape)


def scale_kernel(grad_ref, parts_ref, out_ref):
    total = jnp.sum(parts_ref[...], axis=0, keepdims=True)[:, :1]
    out_ref[...] = grad_ref[...] / jnp.sqrt(total / (D * KVH * 2 * HD) + 1e-06)


def dx_kernel(co_ref, *refs):
    g, wa, wb, out_ref = refs[:8], refs[8:16], refs[16:24], refs[24]
    ca = pl.ds(pl.multiple_of(co_ref[0] * HD, HD), HD)
    cb = pl.ds(pl.multiple_of((1 - co_ref[0]) * HD, HD), HD)
    acc = jnp.zeros((256, 384), jnp.float32)
    for k in range(8):
        acc += lax.dot_general(g[k][:, ca], wa[k][...], NT, preferred_element_type=jnp.float32)
        acc += lax.dot_general(g[k][:, cb], wb[k][...], NT, preferred_element_type=jnp.float32)
    out_ref[...] = acc.astype(jnp.bfloat16)


def dq_kernel(a_ref, b_ref, out_ref):
    for b in range(3):
        for lh in range(NLH):
            cs = slice(lh * HD, (lh + 1) * HD)
            t = a_ref[b, :, cs] + b_ref[b, :, cs].astype(jnp.float32)
            h = lh % 3
            out_ref[lh // 3, b * HD : (b + 1) * HD, h * HD : (h + 1) * HD] = t.T.astype(jnp.bfloat16)


def call(kernel, specs, *shapes):
    out = tuple(jax.ShapeDtypeStruct(s, d) for s, d in shapes)
    return pl.pallas_call(kernel, out_shape=out, in_specs=specs, out_specs=tuple(VM for _ in out))


def swap(a):
    return lax.ppermute(a, "co", [(0, 1), (1, 0)])


DELTAS = [(i, j) for i in range(2) for j in range(4) if (i, j) != (0, 0)]


def shift(a, delta):
    perm = []
    for i in range(2):
        for j in range(4):
            perm.append((4 * i + j, 4 * ((i + delta[0]) % 2) + (j + delta[1]) % 4))
    return lax.ppermute(a, K8, perm)


def exchange(a, axes):
    return lax.all_to_all(a, axes, 0, 0)


def step(x_kv, w_kv, queries, d_out, lse, delta, offsets, block_mask):
    f32 = jnp.float32
    bf = jnp.bfloat16
    co = lax.axis_index("co")
    co1 = co.reshape(1).astype(jnp.int32)
    kv_local = jnp.dot(x_kv, w_kv, preferred_element_type=f32).astype(bf)
    kv_all = exchange(jnp.broadcast_to(kv_local[None], (8, 256, 256)), C8)
    w_half = lax.dynamic_slice_in_dim(w_kv, co * HD, HD, 1).reshape(8, 384, HD)
    xh, z = lax.axis_index("xh"), lax.axis_index("z")
    wa = [lax.dynamic_index_in_dim(w_half, 4 * xh + z, 0, False)]
    for i, j in DELTAS:
        piece = lax.dynamic_index_in_dim(w_half, 4 * ((xh + i) % 2) + (z + j) % 4, 0, False)
        wa.append(shift(piece, (i, j)))
    ints = jnp.concatenate([block_mask.reshape(96), offsets, jnp.zeros((31,), jnp.int32)])
    rows = jnp.concatenate([lse, delta], axis=2).reshape(NL, 3, HD, 2, 3)
    small = jnp.transpose(rows, (1, 3, 0, 4, 2)).reshape(3, 2 * NLH, HD)
    x_t = x_kv.T.reshape(8, 2, 192, 256)
    xa = lax.dynamic_index_in_dim(x_t, co, 1, False)
    xb = swap(lax.dynamic_index_in_dim(x_t, 1 - co, 1, False))
    dkv, dqo, dqp = attn(
        ints, swap(ints), co1, small, swap(small),
        kv_all.reshape(KB, HD, 2 * HD), queries, swap(queries), d_out, swap(d_out),
    )
    dkv_r = exchange(dkv.reshape(8, 256, 256), C8)
    (g,) = call(sum_kernel, [VM], ((256, 256), bf))(dkv_r)
    (dw_part,) = call(dw_kernel, [VM] * 4, ((8, 192, 256), bf))(xa, xb, g, swap(g))
    dw_r = exchange(dw_part, C8)
    grad, sq = call(grad_kernel, [VM], ((192, 256), f32), ((128, HD), f32))(dw_r)
    parts = exchange(sq.reshape(128, 1, HD), ALL)
    gs = [g] + [shift(g, d) for d in DELTAS]
    wb = swap(jnp.stack(wa))
    (d_x,) = call(dx_kernel, [SM] + [VM] * 24, ((256, 384), bf))(
        co1, *gs, *wa, *[wb[k] for k in range(8)]
    )
    (d_queries,) = call(dq_kernel, [VM] * 2, ((NL, 384, 384), bf))(dqo, swap(dqp))
    (d_w,) = call(scale_kernel, [VM] * 2, ((192, 256), f32))(grad, parts.reshape(128, HD))
    return (d_queries, d_x, d_w)


def solution(mesh):
    mesh5 = Mesh(mesh.devices.reshape(2, 4, 2, 2, 4), ALL)
    ctx = ("xl", "y", "co")
    kvh = ("xh", "z")
    in_specs = (
        P(ctx, None),
        P(None, kvh),
        P(None, ctx, kvh),
        P(None, ctx, kvh),
        P(None, ctx, kvh),
        P(None, ctx, kvh),
        P(ctx),
        P(ctx, None),
    )
    out_specs = (P(None, ctx, kvh), P(ctx, kvh), P(ctx, kvh))
    return jax.shard_map(step, mesh=mesh5, in_specs=in_specs, out_specs=out_specs, check_vma=False)
```

```python
import functools

import jax
import jax.numpy as jnp
from jax import lax
from jax.experimental import pallas as pl
from jax.experimental.pallas import tpu as pltpu
from jax.sharding import Mesh, PartitionSpec as P

D = 3072
KVH = 8
HD = 128
NL = 3
NLH = 9
KB = 16
QB = 6
LOG2E = 1.4426950408889634
C1 = LOG2E * HD ** (-0.5)
NEG = -1e30
NT = (((1,), (1,)), ((), ()))
NN = (((1,), (0,)), ((), ()))
C8 = ("xl", "y")
K8 = ("xh", "z")
ALL = ("xl", "y", "co", "xh", "z")


def attn_kernel(groups, ints_o, ints_p, co_ref, small_o, small_p, kv_ref, qo, qp, oo, op, dkv_ref, dqo_ref, dqp_ref,
                q_s, o_s, kT_s, acc_s, dq_s, p_s, ds_s, bias_s, lst, cnt, sem):
    f32=jnp.float32; bf=jnp.bfloat16
    copies=[pltpu.make_async_copy(a, d, sem.at[i]) for i,(a,d) in enumerate(
        [(qo,q_s.at[0]),(oo,o_s.at[0]),(qp,q_s.at[1]),(op,o_s.at[1])])]
    for c in copies: c.start()
    co=co_ref[0]
    acc_s[...]=jnp.zeros(acc_s.shape,f32)
    for kb in range(KB):
        kT_s[kb]=kv_ref[kb,:,:HD].T
    for s,ints in ((0,ints_o),(1,ints_p)):
        off=ints[96]
        for b in range(3):
            n=jnp.int32(0)
            for kb in range(KB):
                j,c=divmod(kb,2)
                i=(j//4)*8+(j%4)*2+co
                st=i*256+c*128
                vis=(ints[b*32+2*i+c]==1)&(st<off+(b*128+127))
                lst[s*3+b,n]=jnp.int32(kb)
                n=n+vis.astype(jnp.int32)
            cnt[s*3+b]=n
            lst[s*3+b,n]=jnp.int32(KB)
    for c in copies: c.wait()

    rowi=lax.broadcasted_iota(jnp.int32,(HD,HD),0)
    coli=lax.broadcasted_iota(jnp.int32,(HD,HD),1)
    dif=coli-rowi

    def qb_body(qb,_):
        s=qb//3; b=qb-3*s
        rows=pl.ds(pl.multiple_of(b*128,128),128)
        n=cnt[qb]
        off=jnp.where(s==0,ints_o[96],ints_p[96])+b*128
        dq_s[...]=jnp.zeros(dq_s.shape,f32)
        def qg(ref,lhs):
            return jnp.concatenate([ref[s,lh//3,rows,(lh%3)*HD:(lh%3+1)*HD] for lh in lhs],axis=0)
        def pair(t,_):
            kb0=lst[qb,2*t]
            kb1r=lst[qb,2*t+1]
            one=2*t+1>=n
            kb1=jnp.where(one,kb0,kb1r)
            def start(kb):
                j=kb//2
                return ((j//4)*8+(j%4)*2+co)*256+(kb-2*j)*128
            st0=start(kb0)
            st1=jnp.where(one,jnp.int32(1<<20),start(kb1))
            bias_s[0:HD]=jnp.where(dif>st0-off,f32(0),f32(NEG))
            bias_s[HD:]=jnp.where(dif>st1-off,f32(0),f32(NEG))
            K2=jnp.concatenate([kv_ref[kb0,:,:HD],kv_ref[kb1,:,:HD]],axis=0)
            V2=jnp.concatenate([kv_ref[kb0,:,HD:],kv_ref[kb1,:,HD:]],axis=0)
            K2T=jnp.concatenate([kT_s[kb0],kT_s[kb1]],axis=1)
            bias=bias_s[...]
            for g in groups:
                Q=qg(q_s,g); O=qg(o_s,g)
                ST=lax.dot_general(K2,Q,NT,preferred_element_type=f32)
                DP=lax.dot_general(V2,O,NT,preferred_element_type=f32)
                for u,lh in enumerate(g):
                    cs=slice(u*HD,(u+1)*HD)
                    lse=jnp.where(s==0,small_o[b,lh],small_p[b,lh])[None,:]*f32(LOG2E)
                    dl=jnp.where(s==0,small_o[b,9+lh],small_p[b,9+lh])[None,:]
                    p=jnp.exp2(ST[:,cs]*f32(C1)-lse+bias)
                    p_s[:,lh*HD:(lh+1)*HD]=p.astype(bf)
                    ds_s[:,lh*HD:(lh+1)*HD]=(p*(DP[:,cs]-dl)).astype(bf)
            allq=tuple(range(NLH))
            dv=lax.dot_general(p_s[...],qg(o_s,allq),NN,preferred_element_type=f32)
            dk=lax.dot_general(ds_s[...],qg(q_s,allq),NN,preferred_element_type=f32)
            acc_s[kb0,:,:HD]+=dk[:HD]
            acc_s[kb0,:,HD:]+=dv[:HD]
            acc_s[kb1,:,:HD]+=dk[HD:]
            acc_s[kb1,:,HD:]+=dv[HD:]
            dq_s[...]+=lax.dot_general(K2T,ds_s[...],NN,preferred_element_type=f32)
            return 0
        lax.fori_loop(0,(n+1)//2,pair,0)
        sc=f32(HD**(-0.5))
        @pl.when(s==0)
        def _(): dqo_ref[b]=dq_s[...]*sc
        @pl.when(s==1)
        def _(): dqp_ref[b]=(dq_s[...]*sc).astype(bf)
        return 0
    lax.fori_loop(0,QB,qb_body,0)
    sc=f32(HD**(-0.5))
    dkv_ref[:,:,:HD]=(acc_s[:,:,:HD]*sc).astype(bf)
    dkv_ref[:,:,HD:]=acc_s[:,:,HD:].astype(bf)


def attn(ints_o,ints_p,co,small_o,small_p,kv,qo,qp,oo,op,groups=((0,1),(2,3),(4,5),(6,7),(8,))):
    f32=jnp.float32; bf=jnp.bfloat16
    S=pl.BlockSpec(memory_space=pltpu.SMEM); V=pl.BlockSpec(memory_space=pltpu.VMEM); A=pl.BlockSpec(memory_space=pl.ANY)
    return pl.pallas_call(
        functools.partial(attn_kernel,groups),
        out_shape=(jax.ShapeDtypeStruct((KB,HD,2*HD),bf),jax.ShapeDtypeStruct((3,HD,NLH*HD),f32),jax.ShapeDtypeStruct((3,HD,NLH*HD),bf)),
        in_specs=[S,S,S,V,V,V,A,A,A,A], out_specs=(V,V,V),
        scratch_shapes=[pltpu.VMEM((2,NL,384,384),bf),pltpu.VMEM((2,NL,384,384),bf),pltpu.VMEM((KB,HD,HD),bf),
            pltpu.VMEM((KB,HD,2*HD),f32),pltpu.VMEM((HD,NLH*HD),f32),pltpu.VMEM((2*HD,NLH*HD),bf),pltpu.VMEM((2*HD,NLH*HD),bf),
            pltpu.VMEM((2*HD,HD),f32),pltpu.SMEM((QB,KB+1),jnp.int32),pltpu.SMEM((QB,),jnp.int32),pltpu.SemaphoreType.DMA((4,))],
        name="attn",
    )(ints_o,ints_p,co,small_o,small_p,kv,qo,qp,oo,op)


VM = pl.BlockSpec(memory_space=pltpu.VMEM)
SM = pl.BlockSpec(memory_space=pltpu.SMEM)


def kv_kernel(x_ref, w_ref, out_ref, acc_ref):
    step = pl.program_id(0)
    part = jnp.dot(x_ref[...], w_ref[...], preferred_element_type=jnp.float32)

    @pl.when(step == 0)
    def _():
        acc_ref[...] = part

    @pl.when(step > 0)
    def _():
        acc_ref[...] += part

    @pl.when(step == pl.num_programs(0) - 1)
    def _():
        kv = acc_ref[...].astype(jnp.bfloat16)
        for k in range(8):
            out_ref[k] = kv


def project(x, w, steps=4):
    depth = D // steps
    return pl.pallas_call(
        kv_kernel,
        grid=(steps,),
        out_shape=jax.ShapeDtypeStruct((8, 256, 256), jnp.bfloat16),
        in_specs=[
            pl.BlockSpec((256, depth), lambda i: (0, i)),
            pl.BlockSpec((depth, 256), lambda i: (i, 0)),
        ],
        out_specs=pl.BlockSpec((8, 256, 256), lambda i: (0, 0, 0)),
        scratch_shapes=[pltpu.VMEM((256, 256), jnp.float32)],
        name="kv",
    )(x, w)


def sum_kernel(r_ref, out_ref):
    acc = r_ref[0].astype(jnp.float32)
    for k in range(1, 8):
        acc += r_ref[k].astype(jnp.float32)
    out_ref[...] = acc.astype(jnp.bfloat16)


def dw_kernel(xa_ref, xb_ref, ga_ref, gb_ref, out_ref):
    for k in range(8):
        acc = lax.dot_general(xa_ref[k], ga_ref[...], NN, preferred_element_type=jnp.float32)
        acc += lax.dot_general(xb_ref[k], gb_ref[...], NN, preferred_element_type=jnp.float32)
        out_ref[k] = acc.astype(jnp.bfloat16)


def grad_kernel(r_ref, grad_ref, sq_ref):
    acc = r_ref[0].astype(jnp.float32)
    for k in range(1, 8):
        acc += r_ref[k].astype(jnp.float32)
    grad_ref[...] = acc
    sq = jnp.sum(jnp.sum(acc * acc, axis=0, keepdims=True), axis=1, keepdims=True)
    sq_ref[...] = jnp.broadcast_to(sq, sq_ref.shape)


def scale_kernel(grad_ref, parts_ref, out_ref):
    total = jnp.sum(parts_ref[...], axis=0, keepdims=True)[:, :1]
    out_ref[...] = grad_ref[...] / jnp.sqrt(total / (D * KVH * 2 * HD) + 1e-06)


def dx_kernel(co_ref, *refs):
    g, wa, wb, out_ref = refs[:8], refs[8:12], refs[12:16], refs[16]

    def total(near, far):
        acc = jnp.zeros((256, 384), jnp.float32)
        for k in range(4):
            acc += lax.dot_general(g[k][...], near[k][...], NT, preferred_element_type=jnp.float32)
            acc += lax.dot_general(g[4 + k][...], far[k][...], NT, preferred_element_type=jnp.float32)
        out_ref[...] = acc.astype(jnp.bfloat16)

    @pl.when(co_ref[0] == 0)
    def _():
        total(wa, wb)

    @pl.when(co_ref[0] == 1)
    def _():
        total(wb, wa)


def dq_kernel(a_ref, b_ref, out_ref):
    for b in range(3):
        for lh in range(NLH):
            cs = slice(lh * HD, (lh + 1) * HD)
            t = a_ref[b, :, cs] + b_ref[b, :, cs].astype(jnp.float32)
            h = lh % 3
            out_ref[lh // 3, b * HD : (b + 1) * HD, h * HD : (h + 1) * HD] = t.T.astype(jnp.bfloat16)


def vm(a):
    return pltpu.with_memory_space_constraint(a, pltpu.VMEM)


def call(kernel, specs, *shapes, near=True):
    kind = pltpu.VMEM if near else jax.ShapeDtypeStruct
    out = tuple(kind(s, d) for s, d in shapes)
    return pl.pallas_call(kernel, out_shape=out, in_specs=specs, out_specs=tuple(VM for _ in out))


def swap(a):
    return lax.ppermute(a, "co", [(0, 1), (1, 0)])


DELTAS = [(i, j) for i in range(2) for j in range(4) if (i, j) != (0, 0)]


def shift(a, delta):
    perm = []
    for i in range(2):
        for j in range(4):
            perm.append((4 * i + j, 4 * ((i + delta[0]) % 2) + (j + delta[1]) % 4))
    return lax.ppermute(a, K8, perm)


def split_shift(a, j):
    perm = []
    for i in range(2):
        for k in range(4):
            if j > 0:
                perm.append((4 * i + k, 4 * i + (k + j) % 4))
            perm.append((8 + 4 * i + k, 8 + 4 * (1 - i) + (k + j) % 4))
    return lax.ppermute(a, ("co", "xh", "z"), perm)


def exchange(a, axes):
    return lax.all_to_all(a, axes, 0, 0)


def step(x_kv, w_kv, queries, d_out, lse, delta, offsets, block_mask):
    f32 = jnp.float32
    bf = jnp.bfloat16
    co = lax.axis_index("co")
    co1 = co.reshape(1).astype(jnp.int32)
    kv_all = exchange(project(x_kv, w_kv), C8)
    xh, z = lax.axis_index("xh"), lax.axis_index("z")
    w_rows = w_kv.reshape(8, 384, 256)
    wa = []
    for j in range(4):
        piece = lax.dynamic_index_in_dim(w_rows, 4 * ((xh + co) % 2) + (z + j) % 4, 0, False)
        got = split_shift(piece, j)
        wa.append(jnp.where(co == 0, piece, got) if j == 0 else got)
    ints = jnp.concatenate([block_mask.reshape(96), offsets, jnp.zeros((31,), jnp.int32)])
    rows = jnp.concatenate([lse, delta], axis=2).reshape(NL, 3, HD, 2, 3)
    small = jnp.transpose(rows, (1, 3, 0, 4, 2)).reshape(3, 2 * NLH, HD)
    x_t = x_kv.T.reshape(8, 2, 192, 256)
    xa = lax.dynamic_index_in_dim(x_t, co, 1, False)
    xb = swap(lax.dynamic_index_in_dim(x_t, 1 - co, 1, False))
    dkv, dqo, dqp = attn(
        ints, swap(ints), co1, vm(small), vm(swap(small)),
        vm(kv_all.reshape(KB, HD, 2 * HD)), queries, swap(queries), d_out, swap(d_out),
    )
    dkv_r = exchange(dkv.reshape(8, 256, 256), C8)
    (g,) = call(sum_kernel, [VM], ((256, 256), bf))(vm(dkv_r))
    (dw_part,) = call(dw_kernel, [VM] * 4, ((8, 192, 256), bf))(vm(xa), vm(xb), g, vm(swap(g)))
    dw_r = exchange(dw_part, C8)
    grad, sq = call(grad_kernel, [VM], ((192, 256), f32), ((128, HD), f32))(vm(dw_r))
    parts = exchange(sq.reshape(128, 1, HD), ALL)
    gs = [g]
    for d in DELTAS:
        gs.append(shift(g, d))
    wb = [swap(w) for w in wa]
    (d_x,) = call(dx_kernel, [SM] + [VM] * 16, ((256, 384), bf), near=False)(
        co1, *map(vm, gs + wa + wb)
    )
    (d_queries,) = call(dq_kernel, [VM] * 2, ((NL, 384, 384), bf), near=False)(
        dqo, swap(dqp)
    )
    (d_w,) = call(scale_kernel, [VM] * 2, ((192, 256), f32), near=False)(grad, vm(parts.reshape(128, HD)))
    return (d_queries, d_x, d_w)


def solution(mesh):
    mesh5 = Mesh(mesh.devices.reshape(2, 4, 2, 2, 4), ALL)
    ctx = ("xl", "y", "co")
    kvh = ("xh", "z")
    in_specs = (
        P(ctx, None),
        P(None, kvh),
        P(None, ctx, kvh),
        P(None, ctx, kvh),
        P(None, ctx, kvh),
        P(None, ctx, kvh),
        P(ctx),
        P(ctx, None),
    )
    out_specs = (P(None, ctx, kvh), P(ctx, kvh), P(ctx, kvh))
    return jax.shard_map(step, mesh=mesh5, in_specs=in_specs, out_specs=out_specs, check_vma=False)
```

```python
import functools

import jax
import jax.numpy as jnp
from jax import lax
from jax.experimental import pallas as pl
from jax.experimental.pallas import tpu as pltpu
from jax.sharding import Mesh, PartitionSpec as P

D = 3072
KVH = 8
HD = 128
NL = 3
NLH = 9
KB = 16
QB = 6
LOG2E = 1.4426950408889634
C1 = LOG2E * HD ** (-0.5)
NEG = -1e30
NT = (((1,), (1,)), ((), ()))
NN = (((1,), (0,)), ((), ()))
C8 = ("xl", "y")
K8 = ("xh", "z")
ALL = ("xl", "y", "co", "xh", "z")


def attn_kernel(groups, unroll, ints_o, ints_p, co_ref, small_o, small_p, kv_ref, qo, qp, oo, op, dkv_ref, dqo_ref, dqp_ref,
                q_s, o_s, kT_s, acc_s, dq_s, sm_s, p_s, ds_s, bias_s, lst, one_s, sem):
    f32 = jnp.float32
    bf = jnp.bfloat16
    copies = [
        pltpu.make_async_copy(a, d, sem.at[i])
        for i, (a, d) in enumerate(
            [(qo, q_s.at[0]), (oo, o_s.at[0]), (qp, q_s.at[1]), (op, o_s.at[1])]
        )
    ]
    for c in copies:
        c.start()
    co = co_ref[0]
    acc_s[...] = jnp.zeros(acc_s.shape, f32)
    dq_s[...] = jnp.zeros(dq_s.shape, f32)
    sm_s[0:3] = small_o[...]
    sm_s[3:6] = small_p[...]
    for kb in range(KB):
        kT_s[kb] = kv_ref[kb, :, :HD].T

    def key_start(kb):
        j = kb // 2
        return ((j // 4) * 8 + (j % 4) * 2 + co) * 256 + (kb - 2 * j) * 128

    def clear(i, _):
        one_s[i] = jnp.int32(0)
        return 0

    lax.fori_loop(0, one_s.shape[0], clear, 0)
    n = jnp.int32(0)
    for s, ints in ((0, ints_o), (1, ints_p)):
        for b in range(3):
            low = ints[96] + b * 128
            n = n + (n & 1)
            for kb in range(KB):
                j, c = divmod(kb, 2)
                gk = 2 * ((j // 4) * 8 + (j % 4) * 2 + co) + c
                vis = (ints[b * 32 + gk] == 1) & (gk * 128 < low + 127)
                lst[n] = jnp.int32((3 * s + b) * KB + kb)
                n = n + vis.astype(jnp.int32)
            lst[n] = jnp.int32((3 * s + b) * KB)
            one_s[n // 2] = n & 1
    items = (n + 1) // 2
    for extra in range(unroll):
        lst[2 * (items + extra)] = jnp.int32(0)
        lst[2 * (items + extra) + 1] = jnp.int32(0)
        one_s[items + extra] = jnp.int32(2)
    for c in copies:
        c.wait()

    dif = lax.broadcasted_iota(jnp.int32, (HD, HD), 1) - lax.broadcasted_iota(jnp.int32, (HD, HD), 0)
    everything = tuple(range(NLH))

    def item(t, slot):
        code = lst[2 * t]
        qb = code // KB
        kb0 = code - qb * KB
        kb1 = lst[2 * t + 1] - qb * KB
        hide = one_s[t]
        kb1 = jnp.where(hide > 0, kb0, kb1)
        s = qb // 3
        b = qb - 3 * s
        low = jnp.where(s == 0, ints_o[96], ints_p[96]) + b * 128
        far = jnp.int32(1 << 20)
        st0 = jnp.where(hide > 1, far, key_start(kb0)) - low
        st1 = jnp.where(hide > 0, far, key_start(kb1)) - low
        bias_s[slot, 0:HD] = jnp.where(dif > st0, f32(0), f32(NEG))
        bias_s[slot, HD:] = jnp.where(dif > st1, f32(0), f32(NEG))
        rows = pl.ds(pl.multiple_of(b * 128, 128), 128)

        def stack(ref, lhs):
            return jnp.concatenate(
                [ref[s, lh // 3, rows, (lh % 3) * HD : (lh % 3 + 1) * HD] for lh in lhs], axis=0
            )

        k2 = jnp.concatenate([kv_ref[kb0, :, :HD], kv_ref[kb1, :, :HD]], axis=0)
        v2 = jnp.concatenate([kv_ref[kb0, :, HD:], kv_ref[kb1, :, HD:]], axis=0)
        for g in groups:
            st = lax.dot_general(k2, stack(q_s, g), NT, preferred_element_type=f32)
            dp = lax.dot_general(v2, stack(o_s, g), NT, preferred_element_type=f32)
            for u, lh in enumerate(g):
                cs = slice(u * HD, (u + 1) * HD)
                out = slice(lh * HD, (lh + 1) * HD)
                lse = sm_s[qb, lh][None, :] * f32(LOG2E)
                p = jnp.exp2(st[:, cs] * f32(C1) - lse + bias_s[slot])
                p_s[slot, :, out] = p.astype(bf)
                ds_s[slot, :, out] = (p * (dp[:, cs] - sm_s[qb, NLH + lh][None, :])).astype(bf)
        dv = lax.dot_general(p_s[slot], stack(o_s, everything), NN, preferred_element_type=f32)
        dk = lax.dot_general(ds_s[slot], stack(q_s, everything), NN, preferred_element_type=f32)
        acc_s[kb0, :, :HD] += dk[:HD]
        acc_s[kb0, :, HD:] += dv[:HD]
        acc_s[kb1, :, :HD] += dk[HD:]
        acc_s[kb1, :, HD:] += dv[HD:]
        k2t = jnp.concatenate([kT_s[kb0], kT_s[kb1]], axis=1)
        dq_s[qb] += lax.dot_general(k2t, ds_s[slot], NN, preferred_element_type=f32)

    def trip(r, _):
        for slot in range(unroll):
            item(r * unroll + slot, slot)
        return 0

    lax.fori_loop(0, (items + unroll - 1) // unroll, trip, 0)
    scale = f32(HD ** (-0.5))
    dqo_ref[...] = dq_s[0:3] * scale
    dqp_ref[...] = (dq_s[3:6] * scale).astype(bf)
    dkv_ref[:, :, :HD] = (acc_s[:, :, :HD] * scale).astype(bf)
    dkv_ref[:, :, HD:] = acc_s[:, :, HD:].astype(bf)


def attn(ints_o, ints_p, co, small_o, small_p, kv, qo, qp, oo, op, groups=((0, 1), (2, 3), (4, 5), (6, 7), (8,)), unroll=2, near=False):
    f32 = jnp.float32
    bf = jnp.bfloat16
    smem = pl.BlockSpec(memory_space=pltpu.SMEM)
    vmem = pl.BlockSpec(memory_space=pltpu.VMEM)
    anym = pl.BlockSpec(memory_space=pl.ANY)
    kind = pltpu.VMEM if near else jax.ShapeDtypeStruct
    return pl.pallas_call(
        functools.partial(attn_kernel, groups, unroll),
        out_shape=(
            jax.ShapeDtypeStruct((KB, HD, 2 * HD), bf),
            kind((3, HD, NLH * HD), f32),
            kind((3, HD, NLH * HD), bf),
        ),
        in_specs=[smem] * 3 + [vmem] * 3 + [anym] * 4,
        out_specs=(vmem, vmem, vmem),
        scratch_shapes=[
            pltpu.VMEM((2, NL, 384, 384), bf),
            pltpu.VMEM((2, NL, 384, 384), bf),
            pltpu.VMEM((KB, HD, HD), bf),
            pltpu.VMEM((KB, HD, 2 * HD), f32),
            pltpu.VMEM((QB, HD, NLH * HD), f32),
            pltpu.VMEM((QB, 2 * NLH, HD), f32),
            pltpu.VMEM((unroll, 2 * HD, NLH * HD), bf),
            pltpu.VMEM((unroll, 2 * HD, NLH * HD), bf),
            pltpu.VMEM((unroll, 2 * HD, HD), f32),
            pltpu.SMEM((QB * KB + 2 * unroll + 2,), jnp.int32),
            pltpu.SMEM((QB * KB // 2 + unroll + 1,), jnp.int32),
            pltpu.SemaphoreType.DMA((4,)),
        ],
        name="attn",
    )(ints_o, ints_p, co, small_o, small_p, kv, qo, qp, oo, op)


VM = pl.BlockSpec(memory_space=pltpu.VMEM)
SM = pl.BlockSpec(memory_space=pltpu.SMEM)


def kv_kernel(x_ref, w_ref, out_ref, acc_ref):
    step = pl.program_id(0)
    part = jnp.dot(x_ref[...], w_ref[...], preferred_element_type=jnp.float32)

    @pl.when(step == 0)
    def _():
        acc_ref[...] = part

    @pl.when(step > 0)
    def _():
        acc_ref[...] += part

    @pl.when(step == pl.num_programs(0) - 1)
    def _():
        kv = acc_ref[...].astype(jnp.bfloat16)
        for k in range(8):
            out_ref[k] = kv


def project(x, w, steps=4):
    depth = D // steps
    return pl.pallas_call(
        kv_kernel,
        grid=(steps,),
        out_shape=jax.ShapeDtypeStruct((8, 256, 256), jnp.bfloat16),
        in_specs=[
            pl.BlockSpec((256, depth), lambda i: (0, i)),
            pl.BlockSpec((depth, 256), lambda i: (i, 0)),
        ],
        out_specs=pl.BlockSpec((8, 256, 256), lambda i: (0, 0, 0)),
        scratch_shapes=[pltpu.VMEM((256, 256), jnp.float32)],
        name="kv",
    )(x, w)


def sum_kernel(r_ref, out_ref):
    acc = r_ref[0].astype(jnp.float32)
    for k in range(1, 8):
        acc += r_ref[k].astype(jnp.float32)
    out_ref[...] = acc.astype(jnp.bfloat16)


def dw_kernel(xa_ref, xb_ref, ga_ref, gb_ref, out_ref):
    for k in range(8):
        acc = lax.dot_general(xa_ref[k], ga_ref[...], NN, preferred_element_type=jnp.float32)
        acc += lax.dot_general(xb_ref[k], gb_ref[...], NN, preferred_element_type=jnp.float32)
        out_ref[k] = acc.astype(jnp.bfloat16)


def grad_kernel(r_ref, grad_ref, sq_ref):
    acc = r_ref[0].astype(jnp.float32)
    for k in range(1, 8):
        acc += r_ref[k].astype(jnp.float32)
    grad_ref[...] = acc
    sq = jnp.sum(jnp.sum(acc * acc, axis=0, keepdims=True), axis=1, keepdims=True)
    sq_ref[...] = jnp.broadcast_to(sq, sq_ref.shape)


def scale_kernel(grad_ref, parts_ref, out_ref):
    total = jnp.sum(parts_ref[...], axis=0, keepdims=True)[:, :1]
    out_ref[...] = grad_ref[...] / jnp.sqrt(total / (D * KVH * 2 * HD) + 1e-06)


def dx_kernel(co_ref, *refs):
    g, wa, wb, out_ref = refs[:8], refs[8:12], refs[12:16], refs[16]

    def total(near, far):
        acc = jnp.zeros((256, 384), jnp.float32)
        for k in range(4):
            acc += lax.dot_general(g[k][...], near[k][...], NT, preferred_element_type=jnp.float32)
            acc += lax.dot_general(g[4 + k][...], far[k][...], NT, preferred_element_type=jnp.float32)
        out_ref[...] = acc.astype(jnp.bfloat16)

    @pl.when(co_ref[0] == 0)
    def _():
        total(wa, wb)

    @pl.when(co_ref[0] == 1)
    def _():
        total(wb, wa)


def dq_kernel(a_ref, b_ref, out_ref):
    for b in range(3):
        for lh in range(NLH):
            cs = slice(lh * HD, (lh + 1) * HD)
            t = a_ref[b, :, cs] + b_ref[b, :, cs].astype(jnp.float32)
            h = lh % 3
            out_ref[lh // 3, b * HD : (b + 1) * HD, h * HD : (h + 1) * HD] = t.T.astype(jnp.bfloat16)


def vm(a):
    return pltpu.with_memory_space_constraint(a, pltpu.VMEM)


def call(kernel, specs, *shapes, near=True):
    kind = pltpu.VMEM if near else jax.ShapeDtypeStruct
    out = tuple(kind(s, d) for s, d in shapes)
    return pl.pallas_call(kernel, out_shape=out, in_specs=specs, out_specs=tuple(VM for _ in out))


def swap(a):
    return lax.ppermute(a, "co", [(0, 1), (1, 0)])


DELTAS = [(i, j) for i in range(2) for j in range(4) if (i, j) != (0, 0)]


def shift(a, delta):
    perm = []
    for i in range(2):
        for j in range(4):
            perm.append((4 * i + j, 4 * ((i + delta[0]) % 2) + (j + delta[1]) % 4))
    return lax.ppermute(a, K8, perm)


def split_shift(a, j):
    perm = []
    for i in range(2):
        for k in range(4):
            if j > 0:
                perm.append((4 * i + k, 4 * i + (k + j) % 4))
            perm.append((8 + 4 * i + k, 8 + 4 * (1 - i) + (k + j) % 4))
    return lax.ppermute(a, ("co", "xh", "z"), perm)


def exchange(a, axes):
    return lax.all_to_all(a, axes, 0, 0)


def step(x_kv, w_kv, queries, d_out, lse, delta, offsets, block_mask):
    f32 = jnp.float32
    bf = jnp.bfloat16
    co = lax.axis_index("co")
    co1 = co.reshape(1).astype(jnp.int32)
    kv_all = exchange(project(x_kv, w_kv), C8)
    xh, z = lax.axis_index("xh"), lax.axis_index("z")
    w_rows = w_kv.reshape(8, 384, 256)
    wa = []
    for j in range(4):
        piece = lax.dynamic_index_in_dim(w_rows, 4 * ((xh + co) % 2) + (z + j) % 4, 0, False)
        got = split_shift(piece, j)
        wa.append(jnp.where(co == 0, piece, got) if j == 0 else got)
    ints = jnp.concatenate([block_mask.reshape(96), offsets, jnp.zeros((31,), jnp.int32)])
    rows = jnp.concatenate([lse, delta], axis=2).reshape(NL, 3, HD, 2, 3)
    small = jnp.transpose(rows, (1, 3, 0, 4, 2)).reshape(3, 2 * NLH, HD)
    x_t = x_kv.T.reshape(8, 2, 192, 256)
    xa = lax.dynamic_index_in_dim(x_t, co, 1, False)
    xb = swap(lax.dynamic_index_in_dim(x_t, 1 - co, 1, False))
    dkv, dqo, dqp = attn(
        ints, swap(ints), co1, vm(small), vm(swap(small)),
        vm(kv_all.reshape(KB, HD, 2 * HD)), queries, swap(queries), d_out, swap(d_out),
    )
    dkv_r = exchange(dkv.reshape(8, 256, 256), C8)
    (g,) = call(sum_kernel, [VM], ((256, 256), bf))(vm(dkv_r))
    (dw_part,) = call(dw_kernel, [VM] * 4, ((8, 192, 256), bf))(vm(xa), vm(xb), g, vm(swap(g)))
    dw_r = exchange(dw_part, C8)
    grad, sq = call(grad_kernel, [VM], ((192, 256), f32), ((128, HD), f32))(vm(dw_r))
    parts = exchange(sq.reshape(128, 1, HD), ALL)
    gs = [g]
    for d in DELTAS:
        gs.append(shift(g, d))
    wb = [swap(w) for w in wa]
    (d_x,) = call(dx_kernel, [SM] + [VM] * 16, ((256, 384), bf), near=False)(
        co1, *map(vm, gs + wa + wb)
    )
    (d_queries,) = call(dq_kernel, [VM] * 2, ((NL, 384, 384), bf), near=False)(
        dqo, vm(swap(dqp))
    )
    (d_w,) = call(scale_kernel, [VM] * 2, ((192, 256), f32), near=False)(vm(grad), vm(parts.reshape(128, HD)))
    return (d_queries, d_x, d_w)


def solution(mesh):
    mesh5 = Mesh(mesh.devices.reshape(2, 4, 2, 2, 4), ALL)
    ctx = ("xl", "y", "co")
    kvh = ("xh", "z")
    in_specs = (
        P(ctx, None),
        P(None, kvh),
        P(None, ctx, kvh),
        P(None, ctx, kvh),
        P(None, ctx, kvh),
        P(None, ctx, kvh),
        P(ctx),
        P(ctx, None),
    )
    out_specs = (P(None, ctx, kvh), P(ctx, kvh), P(ctx, kvh))
    return jax.shard_map(step, mesh=mesh5, in_specs=in_specs, out_specs=out_specs, check_vma=False)
```

```python
import functools

import jax
import jax.numpy as jnp
from jax import lax
from jax.experimental import pallas as pl
from jax.experimental.pallas import tpu as pltpu
from jax.sharding import Mesh, PartitionSpec as P

D = 3072
KVH = 8
HD = 128
NL = 3
NLH = 9
KB = 16
QB = 6
LOG2E = 1.4426950408889634
C1 = LOG2E * HD ** (-0.5)
NEG = -1e30
NT = (((1,), (1,)), ((), ()))
NN = (((1,), (0,)), ((), ()))
C8 = ("xl", "y")
K8 = ("xh", "z")
ALL = ("xl", "y", "co", "xh", "z")


def attn_kernel(groups, unroll, late, ints_o, ints_p, co_ref, small_o, small_p, kv_ref, qo, qp, oo, op, dkv_ref, dqo_ref, dqp_ref,
                q_s, o_s, kT_s, acc_s, dq_s, sm_s, bias_s, lst, one_s, sem):
    f32 = jnp.float32
    bf = jnp.bfloat16
    copies = [
        pltpu.make_async_copy(a, d, sem.at[i])
        for i, (a, d) in enumerate(
            [(qo, q_s.at[0]), (oo, o_s.at[0]), (qp, q_s.at[1]), (op, o_s.at[1])]
        )
    ]
    for c in copies:
        c.start()
    co = co_ref[0]
    acc_s[...] = jnp.zeros(acc_s.shape, f32)
    dq_s[...] = jnp.zeros(dq_s.shape, f32)
    sm_s[0:3] = small_o[...]
    sm_s[3:6] = small_p[...]
    for kb in range(KB):
        kT_s[kb] = kv_ref[kb, :, :HD].T

    def key_start(kb):
        j = kb // 2
        return ((j // 4) * 8 + (j % 4) * 2 + co) * 256 + (kb - 2 * j) * 128

    def clear(i, _):
        one_s[i] = jnp.int32(0)
        return 0

    lax.fori_loop(0, one_s.shape[0], clear, 0)
    n = jnp.int32(0)
    for s, ints in ((0, ints_o), (1, ints_p)):
        for b in range(3):
            low = ints[96] + b * 128
            n = n + (n & 1)
            for kb in range(KB):
                j, c = divmod(kb, 2)
                gk = 2 * ((j // 4) * 8 + (j % 4) * 2 + co) + c
                vis = (ints[b * 32 + gk] == 1) & (gk * 128 < low + 127)
                lst[n] = jnp.int32((3 * s + b) * KB + kb)
                n = n + vis.astype(jnp.int32)
            lst[n] = jnp.int32((3 * s + b) * KB)
            one_s[n // 2] = n & 1
    items = (n + 1) // 2
    for extra in range(unroll):
        lst[2 * (items + extra)] = jnp.int32(0)
        lst[2 * (items + extra) + 1] = jnp.int32(0)
        one_s[items + extra] = jnp.int32(2)
    for c in copies:
        c.wait()

    dif = lax.broadcasted_iota(jnp.int32, (HD, HD), 1) - lax.broadcasted_iota(jnp.int32, (HD, HD), 0)
    everything = tuple(range(NLH))

    def item(t, slot):
        code = lst[2 * t]
        qb = code // KB
        kb0 = code - qb * KB
        kb1 = lst[2 * t + 1] - qb * KB
        hide = one_s[t]
        kb1 = jnp.where(hide > 0, kb0, kb1)
        s = qb // 3
        b = qb - 3 * s
        low = jnp.where(s == 0, ints_o[96], ints_p[96]) + b * 128
        far = jnp.int32(1 << 20)
        st0 = jnp.where(hide > 1, far, key_start(kb0)) - low
        st1 = jnp.where(hide > 0, far, key_start(kb1)) - low
        bias_s[slot, 0:HD] = jnp.where(dif > st0, f32(0), f32(NEG))
        bias_s[slot, HD:] = jnp.where(dif > st1, f32(0), f32(NEG))
        rows = pl.ds(pl.multiple_of(b * 128, 128), 128)

        def stack(ref, lhs):
            return jnp.concatenate(
                [ref[s, lh // 3, rows, (lh % 3) * HD : (lh % 3 + 1) * HD] for lh in lhs], axis=0
            )

        k2 = jnp.concatenate([kv_ref[kb0, :, :HD], kv_ref[kb1, :, :HD]], axis=0)
        v2 = jnp.concatenate([kv_ref[kb0, :, HD:], kv_ref[kb1, :, HD:]], axis=0)
        ps, dss = [], []
        for g in groups:
            st = lax.dot_general(k2, stack(q_s, g), NT, preferred_element_type=f32)
            dp = lax.dot_general(v2, stack(o_s, g), NT, preferred_element_type=f32)
            for u, lh in enumerate(g):
                cs = slice(u * HD, (u + 1) * HD)
                lse = sm_s[qb, lh][None, :] * f32(LOG2E)
                p = jnp.exp2(st[:, cs] * f32(C1) - lse + bias_s[slot])
                ps.append(p.astype(bf))
                dss.append((p * (dp[:, cs] - sm_s[qb, NLH + lh][None, :])).astype(bf))
        pv = jnp.concatenate(ps, axis=1)
        dsv = jnp.concatenate(dss, axis=1)

        def finish():
            dv = lax.dot_general(pv, stack(o_s, everything), NN, preferred_element_type=f32)
            dk = lax.dot_general(dsv, stack(q_s, everything), NN, preferred_element_type=f32)
            acc_s[kb0, :, :HD] += dk[:HD]
            acc_s[kb0, :, HD:] += dv[:HD]
            acc_s[kb1, :, :HD] += dk[HD:]
            acc_s[kb1, :, HD:] += dv[HD:]
            k2t = jnp.concatenate([kT_s[kb0], kT_s[kb1]], axis=1)
            dq_s[qb] += lax.dot_general(k2t, dsv, NN, preferred_element_type=f32)

        return finish

    def trip(r, _):
        last = None
        for slot in range(unroll):
            finish = item(r * unroll + slot, slot)
            if not late:
                finish()
            elif last is not None:
                last()
            last = finish
        if late:
            last()
        return 0

    lax.fori_loop(0, (items + unroll - 1) // unroll, trip, 0)
    scale = f32(HD ** (-0.5))
    dqo_ref[...] = dq_s[0:3] * scale
    dqp_ref[...] = (dq_s[3:6] * scale).astype(bf)
    dkv_ref[:, :, :HD] = (acc_s[:, :, :HD] * scale).astype(bf)
    dkv_ref[:, :, HD:] = acc_s[:, :, HD:].astype(bf)


def attn(ints_o, ints_p, co, small_o, small_p, kv, qo, qp, oo, op, groups=((0, 1), (2, 3), (4, 5), (6, 7), (8,)), unroll=2, late=False, near=False):
    f32 = jnp.float32
    bf = jnp.bfloat16
    smem = pl.BlockSpec(memory_space=pltpu.SMEM)
    vmem = pl.BlockSpec(memory_space=pltpu.VMEM)
    anym = pl.BlockSpec(memory_space=pl.ANY)
    kind = pltpu.VMEM if near else jax.ShapeDtypeStruct
    return pl.pallas_call(
        functools.partial(attn_kernel, groups, unroll, late),
        out_shape=(
            jax.ShapeDtypeStruct((KB, HD, 2 * HD), bf),
            kind((3, HD, NLH * HD), f32),
            kind((3, HD, NLH * HD), bf),
        ),
        in_specs=[smem] * 3 + [vmem] * 3 + [anym] * 4,
        out_specs=(vmem, vmem, vmem),
        scratch_shapes=[
            pltpu.VMEM((2, NL, 384, 384), bf),
            pltpu.VMEM((2, NL, 384, 384), bf),
            pltpu.VMEM((KB, HD, HD), bf),
            pltpu.VMEM((KB, HD, 2 * HD), f32),
            pltpu.VMEM((QB, HD, NLH * HD), f32),
            pltpu.VMEM((QB, 2 * NLH, HD), f32),
            pltpu.VMEM((unroll, 2 * HD, HD), f32),
            pltpu.SMEM((QB * KB + 2 * unroll + 2,), jnp.int32),
            pltpu.SMEM((QB * KB // 2 + unroll + 1,), jnp.int32),
            pltpu.SemaphoreType.DMA((4,)),
        ],
        name="attn",
    )(ints_o, ints_p, co, small_o, small_p, kv, qo, qp, oo, op)


VM = pl.BlockSpec(memory_space=pltpu.VMEM)
SM = pl.BlockSpec(memory_space=pltpu.SMEM)


def kv_kernel(x_ref, w_ref, out_ref, acc_ref):
    step = pl.program_id(0)
    part = jnp.dot(x_ref[...], w_ref[...], preferred_element_type=jnp.float32)

    @pl.when(step == 0)
    def _():
        acc_ref[...] = part

    @pl.when(step > 0)
    def _():
        acc_ref[...] += part

    @pl.when(step == pl.num_programs(0) - 1)
    def _():
        kv = acc_ref[...].astype(jnp.bfloat16)
        for k in range(8):
            out_ref[k] = kv


def project(x, w, steps=2):
    depth = D // steps
    return pl.pallas_call(
        kv_kernel,
        grid=(steps,),
        out_shape=jax.ShapeDtypeStruct((8, 256, 256), jnp.bfloat16),
        in_specs=[
            pl.BlockSpec((256, depth), lambda i: (0, i)),
            pl.BlockSpec((depth, 256), lambda i: (i, 0)),
        ],
        out_specs=pl.BlockSpec((8, 256, 256), lambda i: (0, 0, 0)),
        scratch_shapes=[pltpu.VMEM((256, 256), jnp.float32)],
        name="kv",
    )(x, w)


def sum_kernel(r_ref, out_ref):
    acc = r_ref[0].astype(jnp.float32)
    for k in range(1, 8):
        acc += r_ref[k].astype(jnp.float32)
    out_ref[...] = acc.astype(jnp.bfloat16)


def dw_kernel(xa_ref, xb_ref, ga_ref, gb_ref, out_ref, near_ref, sem):
    g = jnp.concatenate([ga_ref[...], gb_ref[...]], axis=0)
    copies = []
    for k in range(8):
        x = jnp.concatenate([xa_ref[k], xb_ref[k]], axis=1)
        near_ref[k] = jnp.dot(x, g, preferred_element_type=jnp.float32).astype(jnp.bfloat16)
        copy = pltpu.make_async_copy(near_ref.at[k], out_ref.at[k], sem.at[k])
        copy.start()
        copies.append(copy)
    for copy in copies:
        copy.wait()


def weight_parts(xa, xb, ga, gb):
    return pl.pallas_call(
        dw_kernel,
        out_shape=jax.ShapeDtypeStruct((8, 192, 256), jnp.bfloat16),
        in_specs=[pl.BlockSpec(memory_space=pltpu.VMEM)] * 4,
        out_specs=pl.BlockSpec(memory_space=pl.ANY),
        scratch_shapes=[
            pltpu.VMEM((8, 192, 256), jnp.bfloat16),
            pltpu.SemaphoreType.DMA((8,)),
        ],
        name="dw",
    )(xa, xb, ga, gb)


def grad_kernel(r_ref, grad_ref, sq_ref):
    acc = r_ref[0].astype(jnp.float32)
    for k in range(1, 8):
        acc += r_ref[k].astype(jnp.float32)
    grad_ref[...] = acc
    sq = jnp.sum(jnp.sum(acc * acc, axis=0, keepdims=True), axis=1, keepdims=True)
    sq_ref[...] = jnp.broadcast_to(sq, sq_ref.shape)


def scale_kernel(grad_ref, parts_ref, out_ref):
    total = jnp.sum(parts_ref[...], axis=0, keepdims=True)[:, :1]
    out_ref[...] = grad_ref[...] / jnp.sqrt(total / (D * KVH * 2 * HD) + 1e-06)


def dx_kernel(co_ref, *refs):
    g, wa, wb, out_ref = refs[:8], refs[8:12], refs[12:16], refs[16]

    def total(near, far):
        acc = jnp.zeros((256, 384), jnp.float32)
        for k in range(4):
            acc += lax.dot_general(g[k][...], near[k][...], NT, preferred_element_type=jnp.float32)
            acc += lax.dot_general(g[4 + k][...], far[k][...], NT, preferred_element_type=jnp.float32)
        out_ref[...] = acc.astype(jnp.bfloat16)

    @pl.when(co_ref[0] == 0)
    def _():
        total(wa, wb)

    @pl.when(co_ref[0] == 1)
    def _():
        total(wb, wa)


def dq_kernel(a_ref, b_ref, out_ref):
    for b in range(3):
        for lh in range(NLH):
            cs = slice(lh * HD, (lh + 1) * HD)
            t = a_ref[b, :, cs] + b_ref[b, :, cs].astype(jnp.float32)
            h = lh % 3
            out_ref[lh // 3, b * HD : (b + 1) * HD, h * HD : (h + 1) * HD] = t.T.astype(jnp.bfloat16)


def vm(a):
    return pltpu.with_memory_space_constraint(a, pltpu.VMEM)


def call(kernel, specs, *shapes, near=True):
    kind = pltpu.VMEM if near else jax.ShapeDtypeStruct
    out = tuple(kind(s, d) for s, d in shapes)
    return pl.pallas_call(kernel, out_shape=out, in_specs=specs, out_specs=tuple(VM for _ in out))


def swap(a):
    return lax.ppermute(a, "co", [(0, 1), (1, 0)])


DELTAS = [(i, j) for i in range(2) for j in range(4) if (i, j) != (0, 0)]


def shift(a, delta):
    perm = []
    for i in range(2):
        for j in range(4):
            perm.append((4 * i + j, 4 * ((i + delta[0]) % 2) + (j + delta[1]) % 4))
    return lax.ppermute(a, K8, perm)


def split_shift(a, j):
    perm = []
    for i in range(2):
        for k in range(4):
            if j > 0:
                perm.append((4 * i + k, 4 * i + (k + j) % 4))
            perm.append((8 + 4 * i + k, 8 + 4 * (1 - i) + (k + j) % 4))
    return lax.ppermute(a, ("co", "xh", "z"), perm)


def exchange(a, axes):
    return lax.all_to_all(a, axes, 0, 0)


def step(x_kv, w_kv, queries, d_out, lse, delta, offsets, block_mask):
    f32 = jnp.float32
    bf = jnp.bfloat16
    co = lax.axis_index("co")
    co1 = co.reshape(1).astype(jnp.int32)
    kv_all = exchange(project(x_kv, w_kv), C8)
    xh, z = lax.axis_index("xh"), lax.axis_index("z")
    w_rows = w_kv.reshape(8, 384, 256)
    wa = []
    for j in range(4):
        piece = lax.dynamic_index_in_dim(w_rows, 4 * ((xh + co) % 2) + (z + j) % 4, 0, False)
        got = split_shift(piece, j)
        wa.append(jnp.where(co == 0, piece, got) if j == 0 else got)
    ints = jnp.concatenate([block_mask.reshape(96), offsets, jnp.zeros((31,), jnp.int32)])
    rows = jnp.concatenate([lse, delta], axis=2).reshape(NL, 3, HD, 2, 3)
    small = jnp.transpose(rows, (1, 3, 0, 4, 2)).reshape(3, 2 * NLH, HD)
    x_t = x_kv.T.reshape(8, 2, 192, 256)
    xa = lax.dynamic_index_in_dim(x_t, co, 1, False)
    xb = swap(lax.dynamic_index_in_dim(x_t, 1 - co, 1, False))
    dkv, dqo, dqp = attn(
        ints, swap(ints), co1, vm(small), vm(swap(small)),
        vm(kv_all.reshape(KB, HD, 2 * HD)), queries, swap(queries), d_out, swap(d_out),
    )
    dkv_r = exchange(dkv.reshape(8, 256, 256), C8)
    (g,) = call(sum_kernel, [VM], ((256, 256), bf))(vm(dkv_r))
    dw_part = weight_parts(vm(xa), vm(xb), g, vm(swap(g)))
    dw_r = exchange(dw_part, C8)
    grad, sq = call(grad_kernel, [VM], ((192, 256), f32), ((128, HD), f32))(vm(dw_r))
    parts = exchange(sq.reshape(128, 1, HD), ALL)
    gs = [g]
    for d in DELTAS:
        gs.append(shift(g, d))
    wb = [swap(w) for w in wa]
    (d_x,) = call(dx_kernel, [SM] + [VM] * 16, ((256, 384), bf), near=False)(
        co1, *map(vm, gs + wa + wb)
    )
    (d_queries,) = call(dq_kernel, [VM] * 2, ((NL, 384, 384), bf), near=False)(dqo, vm(swap(dqp)))
    (d_w,) = call(scale_kernel, [VM] * 2, ((192, 256), f32), near=False)(vm(grad), vm(parts.reshape(128, HD)))
    return (d_queries, d_x, d_w)


def solution(mesh):
    mesh5 = Mesh(mesh.devices.reshape(2, 4, 2, 2, 4), ALL)
    ctx = ("xl", "y", "co")
    kvh = ("xh", "z")
    in_specs = (
        P(ctx, None),
        P(None, kvh),
        P(None, ctx, kvh),
        P(None, ctx, kvh),
        P(None, ctx, kvh),
        P(None, ctx, kvh),
        P(ctx),
        P(ctx, None),
    )
    out_specs = (P(None, ctx, kvh), P(ctx, kvh), P(ctx, kvh))
    return jax.shard_map(step, mesh=mesh5, in_specs=in_specs, out_specs=out_specs, check_vma=False)
```

```python
import functools

import jax
import jax.numpy as jnp
from jax import lax
from jax.experimental import pallas as pl
from jax.experimental.pallas import tpu as pltpu
from jax.sharding import Mesh, PartitionSpec as P

D = 3072
KVH = 8
HD = 128
NL = 3
NLH = 9
KB = 16
QB = 6
LOG2E = 1.4426950408889634
C1 = LOG2E * HD ** (-0.5)
NEG = -1e30
NT = (((1,), (1,)), ((), ()))
NN = (((1,), (0,)), ((), ()))
C8 = ("xl", "y")
K8 = ("xh", "z")
ALL = ("xl", "y", "co", "xh", "z")


def attn_kernel(groups, unroll, late, ints_o, ints_p, co_ref, small_o, small_p, kv_ref, qo, qp, oo, op, dkv_ref, dqo_ref, dqp_ref,
                q_s, o_s, kT_s, acc_s, dq_s, sm_s, bias_s, lst, one_s, sem):
    f32 = jnp.float32
    bf = jnp.bfloat16
    copies = [
        pltpu.make_async_copy(a, d, sem.at[i])
        for i, (a, d) in enumerate(
            [(qo, q_s.at[0]), (oo, o_s.at[0]), (qp, q_s.at[1]), (op, o_s.at[1])]
        )
    ]
    for c in copies:
        c.start()
    co = co_ref[0]
    acc_s[...] = jnp.zeros(acc_s.shape, f32)
    dq_s[...] = jnp.zeros(dq_s.shape, f32)
    sm_s[0:3] = small_o[...]
    sm_s[3:6] = small_p[...]
    for kb in range(KB):
        kT_s[kb] = kv_ref[kb, :, :HD].T

    def key_start(kb):
        j = kb // 2
        return ((j // 4) * 8 + (j % 4) * 2 + co) * 256 + (kb - 2 * j) * 128

    def clear(i, _):
        one_s[i] = jnp.int32(0)
        return 0

    lax.fori_loop(0, one_s.shape[0], clear, 0)
    n = jnp.int32(0)
    for s, ints in ((0, ints_o), (1, ints_p)):
        for b in range(3):
            low = ints[96] + b * 128
            n = n + (n & 1)
            for kb in range(KB):
                j, c = divmod(kb, 2)
                gk = 2 * ((j // 4) * 8 + (j % 4) * 2 + co) + c
                vis = (ints[b * 32 + gk] == 1) & (gk * 128 < low + 127)
                lst[n] = jnp.int32((3 * s + b) * KB + kb)
                n = n + vis.astype(jnp.int32)
            lst[n] = jnp.int32((3 * s + b) * KB)
            one_s[n // 2] = n & 1
    items = (n + 1) // 2
    for extra in range(unroll):
        lst[2 * (items + extra)] = jnp.int32(0)
        lst[2 * (items + extra) + 1] = jnp.int32(0)
        one_s[items + extra] = jnp.int32(2)
    for c in copies:
        c.wait()

    dif = lax.broadcasted_iota(jnp.int32, (HD, HD), 1) - lax.broadcasted_iota(jnp.int32, (HD, HD), 0)
    everything = tuple(range(NLH))

    def item(t, slot):
        code = lst[2 * t]
        qb = code // KB
        kb0 = code - qb * KB
        kb1 = lst[2 * t + 1] - qb * KB
        hide = one_s[t]
        kb1 = jnp.where(hide > 0, kb0, kb1)
        s = qb // 3
        b = qb - 3 * s
        low = jnp.where(s == 0, ints_o[96], ints_p[96]) + b * 128
        far = jnp.int32(1 << 20)
        st0 = jnp.where(hide > 1, far, key_start(kb0)) - low
        st1 = jnp.where(hide > 0, far, key_start(kb1)) - low
        bias_s[slot, 0:HD] = jnp.where(dif > st0, f32(0), f32(NEG))
        bias_s[slot, HD:] = jnp.where(dif > st1, f32(0), f32(NEG))
        rows = pl.ds(pl.multiple_of(b * 128, 128), 128)

        def stack(ref, lhs):
            return jnp.concatenate(
                [ref[s, lh // 3, rows, (lh % 3) * HD : (lh % 3 + 1) * HD] for lh in lhs], axis=0
            )

        k2 = jnp.concatenate([kv_ref[kb0, :, :HD], kv_ref[kb1, :, :HD]], axis=0)
        v2 = jnp.concatenate([kv_ref[kb0, :, HD:], kv_ref[kb1, :, HD:]], axis=0)
        ps, dss = [], []
        for g in groups:
            st = lax.dot_general(k2, stack(q_s, g), NT, preferred_element_type=f32)
            dp = lax.dot_general(v2, stack(o_s, g), NT, preferred_element_type=f32)
            for u, lh in enumerate(g):
                cs = slice(u * HD, (u + 1) * HD)
                lse = sm_s[qb, lh][None, :] * f32(LOG2E)
                p = jnp.exp2(st[:, cs] * f32(C1) - lse + bias_s[slot])
                ps.append(p.astype(bf))
                dss.append((p * (dp[:, cs] - sm_s[qb, NLH + lh][None, :])).astype(bf))
        pv = jnp.concatenate(ps, axis=1)
        dsv = jnp.concatenate(dss, axis=1)

        def finish():
            dv = lax.dot_general(pv, stack(o_s, everything), NN, preferred_element_type=f32)
            dk = lax.dot_general(dsv, stack(q_s, everything), NN, preferred_element_type=f32)
            acc_s[kb0, :, :HD] += dk[:HD]
            acc_s[kb0, :, HD:] += dv[:HD]
            acc_s[kb1, :, :HD] += dk[HD:]
            acc_s[kb1, :, HD:] += dv[HD:]
            k2t = jnp.concatenate([kT_s[kb0], kT_s[kb1]], axis=1)
            dq_s[qb] += lax.dot_general(k2t, dsv, NN, preferred_element_type=f32)

        return finish

    def trip(r, _):
        last = None
        for slot in range(unroll):
            finish = item(r * unroll + slot, slot)
            if not late:
                finish()
            elif last is not None:
                last()
            last = finish
        if late:
            last()
        return 0

    lax.fori_loop(0, (items + unroll - 1) // unroll, trip, 0)
    scale = f32(HD ** (-0.5))
    dqo_ref[...] = dq_s[0:3] * scale
    dqp_ref[...] = (dq_s[3:6] * scale).astype(bf)
    dkv_ref[:, :, :HD] = (acc_s[:, :, :HD] * scale).astype(bf)
    dkv_ref[:, :, HD:] = acc_s[:, :, HD:].astype(bf)


def attn(ints_o, ints_p, co, small_o, small_p, kv, qo, qp, oo, op, groups=((0, 1), (2, 3), (4, 5), (6, 7), (8,)), unroll=2, late=False, near=False):
    f32 = jnp.float32
    bf = jnp.bfloat16
    smem = pl.BlockSpec(memory_space=pltpu.SMEM)
    vmem = pl.BlockSpec(memory_space=pltpu.VMEM)
    anym = pl.BlockSpec(memory_space=pl.ANY)
    kind = pltpu.VMEM if near else jax.ShapeDtypeStruct
    return pl.pallas_call(
        functools.partial(attn_kernel, groups, unroll, late),
        out_shape=(
            jax.ShapeDtypeStruct((KB, HD, 2 * HD), bf),
            kind((3, HD, NLH * HD), f32),
            kind((3, HD, NLH * HD), bf),
        ),
        in_specs=[smem] * 3 + [vmem] * 3 + [anym] * 4,
        out_specs=(vmem, vmem, vmem),
        scratch_shapes=[
            pltpu.VMEM((2, NL, 384, 384), bf),
            pltpu.VMEM((2, NL, 384, 384), bf),
            pltpu.VMEM((KB, HD, HD), bf),
            pltpu.VMEM((KB, HD, 2 * HD), f32),
            pltpu.VMEM((QB, HD, NLH * HD), f32),
            pltpu.VMEM((QB, 2 * NLH, HD), f32),
            pltpu.VMEM((unroll, 2 * HD, HD), f32),
            pltpu.SMEM((QB * KB + 2 * unroll + 2,), jnp.int32),
            pltpu.SMEM((QB * KB // 2 + unroll + 1,), jnp.int32),
            pltpu.SemaphoreType.DMA((4,)),
        ],
        name="attn",
    )(ints_o, ints_p, co, small_o, small_p, kv, qo, qp, oo, op)


VM = pl.BlockSpec(memory_space=pltpu.VMEM)
SM = pl.BlockSpec(memory_space=pltpu.SMEM)
ANY = pl.BlockSpec(memory_space=pl.ANY)


def kv_kernel(x_ref, w_ref, out_ref, acc_ref):
    step = pl.program_id(0)
    part = jnp.dot(x_ref[...], w_ref[...], preferred_element_type=jnp.float32)

    @pl.when(step == 0)
    def _():
        acc_ref[...] = part

    @pl.when(step > 0)
    def _():
        acc_ref[...] += part

    @pl.when(step == pl.num_programs(0) - 1)
    def _():
        kv = acc_ref[...].astype(jnp.bfloat16)
        for k in range(8):
            out_ref[k] = kv


def project(x, w, steps=2):
    depth = D // steps
    return pl.pallas_call(
        kv_kernel,
        grid=(steps,),
        out_shape=jax.ShapeDtypeStruct((8, 256, 256), jnp.bfloat16),
        in_specs=[
            pl.BlockSpec((256, depth), lambda i: (0, i)),
            pl.BlockSpec((depth, 256), lambda i: (i, 0)),
        ],
        out_specs=pl.BlockSpec((8, 256, 256), lambda i: (0, 0, 0)),
        scratch_shapes=[pltpu.VMEM((256, 256), jnp.float32)],
        name="kv",
    )(x, w)


def sum_kernel(r_ref, out_ref):
    acc = r_ref[0].astype(jnp.float32)
    for k in range(1, 8):
        acc += r_ref[k].astype(jnp.float32)
    out_ref[...] = acc.astype(jnp.bfloat16)


def xt_kernel(co_ref, x_ref, mine_ref, other_ref, flip_ref):
    mine = pl.ds(pl.multiple_of(co_ref[0] * 192, 64), 192)
    other = pl.ds(pl.multiple_of((1 - co_ref[0]) * 192, 64), 192)
    for k in range(8):
        flip_ref[k] = x_ref[:, k * 384 : (k + 1) * 384].T
        mine_ref[k] = flip_ref[k, mine]
        other_ref[k] = flip_ref[k, other]


def split_tokens(co, x):
    part = jax.ShapeDtypeStruct((8, 192, 256), jnp.bfloat16)
    return pl.pallas_call(
        xt_kernel,
        out_shape=(part, part),
        in_specs=[SM, VM],
        out_specs=(VM, VM),
        scratch_shapes=[pltpu.VMEM((8, 384, 256), jnp.bfloat16)],
        name="xt",
    )(co, x)


def dw_kernel(xa_ref, xb_ref, ga_ref, gb_ref, out_ref, near_ref, sem):
    g = jnp.concatenate([ga_ref[...], gb_ref[...]], axis=0)
    copies = []
    for k in range(8):
        x = jnp.concatenate([xa_ref[k], xb_ref[k]], axis=1)
        near_ref[k] = jnp.dot(x, g, preferred_element_type=jnp.float32).astype(jnp.bfloat16)
        copy = pltpu.make_async_copy(near_ref.at[k], out_ref.at[k], sem.at[k])
        copy.start()
        copies.append(copy)
    for copy in copies:
        copy.wait()


def weight_parts(xa, xb, ga, gb):
    return pl.pallas_call(
        dw_kernel,
        out_shape=jax.ShapeDtypeStruct((8, 192, 256), jnp.bfloat16),
        in_specs=[pl.BlockSpec(memory_space=pltpu.VMEM)] * 4,
        out_specs=pl.BlockSpec(memory_space=pl.ANY),
        scratch_shapes=[
            pltpu.VMEM((8, 192, 256), jnp.bfloat16),
            pltpu.SemaphoreType.DMA((8,)),
        ],
        compiler_params=pltpu.CompilerParams(vmem_limit_bytes=20 << 20),
        name="dw",
    )(xa, xb, ga, gb)


def grad_kernel(r_ref, grad_ref, sq_ref):
    acc = r_ref[0].astype(jnp.float32)
    for k in range(1, 8):
        acc += r_ref[k].astype(jnp.float32)
    grad_ref[...] = acc
    sq = jnp.sum(jnp.sum(acc * acc, axis=0, keepdims=True), axis=1, keepdims=True)
    sq_ref[...] = jnp.broadcast_to(sq, sq_ref.shape)


def scale_kernel(grad_ref, parts_ref, out_ref):
    total = jnp.sum(parts_ref[...], axis=0, keepdims=True)[:, :1]
    out_ref[...] = grad_ref[...] / jnp.sqrt(total / (D * KVH * 2 * HD) + 1e-06)


def dx_kernel(co_ref, *refs):
    g, wa, wb, out_ref = refs[:8], refs[8:12], refs[12:16], refs[16]

    def total(near, far):
        acc = jnp.zeros((256, 384), jnp.float32)
        for k in range(4):
            acc += lax.dot_general(g[k][...], near[k][...], NT, preferred_element_type=jnp.float32)
            acc += lax.dot_general(g[4 + k][...], far[k][...], NT, preferred_element_type=jnp.float32)
        out_ref[...] = acc.astype(jnp.bfloat16)

    @pl.when(co_ref[0] == 0)
    def _():
        total(wa, wb)

    @pl.when(co_ref[0] == 1)
    def _():
        total(wb, wa)


def dq_kernel(a_ref, b_ref, w0, w1, w2, w3, out_ref):
    del w0, w1, w2, w3
    for b in range(3):
        for lh in range(NLH):
            cs = slice(lh * HD, (lh + 1) * HD)
            t = a_ref[b, :, cs] + b_ref[b, :, cs].astype(jnp.float32)
            h = lh % 3
            out_ref[lh // 3, b * HD : (b + 1) * HD, h * HD : (h + 1) * HD] = t.T.astype(jnp.bfloat16)


def vm(a):
    return pltpu.with_memory_space_constraint(a, pltpu.VMEM)


def call(kernel, specs, *shapes, near=True):
    kind = pltpu.VMEM if near else jax.ShapeDtypeStruct
    out = tuple(kind(s, d) for s, d in shapes)
    return pl.pallas_call(kernel, out_shape=out, in_specs=specs, out_specs=tuple(VM for _ in out))


def swap(a):
    return lax.ppermute(a, "co", [(0, 1), (1, 0)])


DELTAS = [(i, j) for i in range(2) for j in range(4) if (i, j) != (0, 0)]


def shift(a, delta):
    perm = []
    for i in range(2):
        for j in range(4):
            perm.append((4 * i + j, 4 * ((i + delta[0]) % 2) + (j + delta[1]) % 4))
    return lax.ppermute(a, K8, perm)


def split_shift(a, j):
    perm = []
    for i in range(2):
        for k in range(4):
            if j > 0:
                perm.append((4 * i + k, 4 * i + (k + j) % 4))
            perm.append((8 + 4 * i + k, 8 + 4 * (1 - i) + (k + j) % 4))
    return lax.ppermute(a, ("co", "xh", "z"), perm)


def exchange(a, axes):
    return lax.all_to_all(a, axes, 0, 0)


def step(x_kv, w_kv, queries, d_out, lse, delta, offsets, block_mask):
    f32 = jnp.float32
    bf = jnp.bfloat16
    co = lax.axis_index("co")
    co1 = co.reshape(1).astype(jnp.int32)
    kv_all = exchange(project(x_kv, w_kv), C8)
    xh, z = lax.axis_index("xh"), lax.axis_index("z")
    w_rows = w_kv.reshape(8, 384, 256)
    wa = []
    for j in range(4):
        piece = lax.dynamic_index_in_dim(w_rows, 4 * ((xh + co) % 2) + (z + j) % 4, 0, False)
        got = split_shift(piece, j)
        wa.append(jnp.where(co == 0, piece, got) if j == 0 else got)
    ints = jnp.concatenate([block_mask.reshape(96), offsets, jnp.zeros((31,), jnp.int32)])
    rows = jnp.concatenate([lse, delta], axis=2).reshape(NL, 3, HD, 2, 3)
    small = jnp.transpose(rows, (1, 3, 0, 4, 2)).reshape(3, 2 * NLH, HD)
    xa, xb = split_tokens(co1, x_kv)
    xb = swap(xb)
    dkv, dqo, dqp = attn(
        ints, swap(ints), co1, vm(small), vm(swap(small)),
        vm(kv_all.reshape(KB, HD, 2 * HD)), queries, swap(queries), d_out, swap(d_out),
    )
    dkv_r = exchange(dkv.reshape(8, 256, 256), C8)
    (g,) = call(sum_kernel, [VM], ((256, 256), bf))(vm(dkv_r))
    dw_part = weight_parts(vm(xa), vm(xb), g, vm(swap(g)))
    dw_r = exchange(dw_part, C8)
    grad, sq = call(grad_kernel, [VM], ((192, 256), f32), ((128, HD), f32))(vm(dw_r))
    parts = exchange(sq.reshape(128, 1, HD), ALL)
    gs = [g]
    for d in DELTAS:
        gs.append(shift(g, d))
    wb = [swap(w) for w in wa]
    (d_x,) = call(dx_kernel, [SM] + [VM] * 16, ((256, 384), bf), near=False)(
        co1, *map(vm, gs + wa + wb)
    )
    (d_queries,) = call(dq_kernel, [VM] * 2 + [ANY] * 4, ((NL, 384, 384), bf), near=False)(
        dqo, vm(swap(dqp)), *wb
    )
    (d_w,) = call(scale_kernel, [VM] * 2, ((192, 256), f32), near=False)(vm(grad), vm(parts.reshape(128, HD)))
    return (d_queries, d_x, d_w)


def solution(mesh):
    mesh5 = Mesh(mesh.devices.reshape(2, 4, 2, 2, 4), ALL)
    ctx = ("xl", "y", "co")
    kvh = ("xh", "z")
    in_specs = (
        P(ctx, None),
        P(None, kvh),
        P(None, ctx, kvh),
        P(None, ctx, kvh),
        P(None, ctx, kvh),
        P(None, ctx, kvh),
        P(ctx),
        P(ctx, None),
    )
    out_specs = (P(None, ctx, kvh), P(ctx, kvh), P(ctx, kvh))
    return jax.shard_map(step, mesh=mesh5, in_specs=in_specs, out_specs=out_specs, check_vma=False)
```

```python
import functools

import jax
import jax.numpy as jnp
from jax import lax
from jax.experimental import pallas as pl
from jax.experimental.pallas import tpu as pltpu
from jax.sharding import Mesh, PartitionSpec as P

D = 3072
KVH = 8
HD = 128
NL = 3
NLH = 9
KB = 16
QB = 6
LOG2E = 1.4426950408889634
C1 = LOG2E * HD ** (-0.5)
NEG = -1e30
NT = (((1,), (1,)), ((), ()))
NN = (((1,), (0,)), ((), ()))
C8 = ("xl", "y")
ALL = ("xl", "y", "co", "xh", "z")


def attn_kernel(groups, unroll, late, ints_o, ints_p, co_ref, small_o, small_p, kv_ref, qo, qp, oo, op, dkv_ref, dqo_ref, dqp_ref,
                q_s, o_s, kT_s, acc_s, dq_s, sm_s, bias_s, lst, one_s, sem):
    f32 = jnp.float32
    bf = jnp.bfloat16
    copies = [
        pltpu.make_async_copy(a, d, sem.at[i])
        for i, (a, d) in enumerate(
            [(qo, q_s.at[0]), (oo, o_s.at[0]), (qp, q_s.at[1]), (op, o_s.at[1])]
        )
    ]
    for c in copies:
        c.start()
    co = co_ref[0]
    acc_s[...] = jnp.zeros(acc_s.shape, f32)
    dq_s[...] = jnp.zeros(dq_s.shape, f32)
    sm_s[0:3] = small_o[...]
    sm_s[3:6] = small_p[...]
    for kb in range(KB):
        kT_s[kb] = kv_ref[kb, :, :HD].T

    def key_start(kb):
        j = kb // 2
        return ((j // 4) * 8 + (j % 4) * 2 + co) * 256 + (kb - 2 * j) * 128

    def clear(i, _):
        one_s[i] = jnp.int32(0)
        return 0

    lax.fori_loop(0, one_s.shape[0], clear, 0)
    n = jnp.int32(0)
    for s, ints in ((0, ints_o), (1, ints_p)):
        for b in range(3):
            low = ints[96] + b * 128
            n = n + (n & 1)
            for kb in range(KB):
                j, c = divmod(kb, 2)
                gk = 2 * ((j // 4) * 8 + (j % 4) * 2 + co) + c
                vis = (ints[b * 32 + gk] == 1) & (gk * 128 < low + 127)
                lst[n] = jnp.int32((3 * s + b) * KB + kb)
                n = n + vis.astype(jnp.int32)
            lst[n] = jnp.int32((3 * s + b) * KB)
            one_s[n // 2] = n & 1
    items = (n + 1) // 2
    for extra in range(unroll):
        lst[2 * (items + extra)] = jnp.int32(0)
        lst[2 * (items + extra) + 1] = jnp.int32(0)
        one_s[items + extra] = jnp.int32(2)
    for c in copies:
        c.wait()

    dif = lax.broadcasted_iota(jnp.int32, (HD, HD), 1) - lax.broadcasted_iota(jnp.int32, (HD, HD), 0)
    everything = tuple(range(NLH))

    def item(t, slot):
        code = lst[2 * t]
        qb = code // KB
        kb0 = code - qb * KB
        kb1 = lst[2 * t + 1] - qb * KB
        hide = one_s[t]
        kb1 = jnp.where(hide > 0, kb0, kb1)
        s = qb // 3
        b = qb - 3 * s
        low = jnp.where(s == 0, ints_o[96], ints_p[96]) + b * 128
        far = jnp.int32(1 << 20)
        st0 = jnp.where(hide > 1, far, key_start(kb0)) - low
        st1 = jnp.where(hide > 0, far, key_start(kb1)) - low
        bias_s[slot, 0:HD] = jnp.where(dif > st0, f32(0), f32(NEG))
        bias_s[slot, HD:] = jnp.where(dif > st1, f32(0), f32(NEG))
        rows = pl.ds(pl.multiple_of(b * 128, 128), 128)

        def stack(ref, lhs):
            return jnp.concatenate(
                [ref[s, lh // 3, rows, (lh % 3) * HD : (lh % 3 + 1) * HD] for lh in lhs], axis=0
            )

        k2 = jnp.concatenate([kv_ref[kb0, :, :HD], kv_ref[kb1, :, :HD]], axis=0)
        v2 = jnp.concatenate([kv_ref[kb0, :, HD:], kv_ref[kb1, :, HD:]], axis=0)
        ps, dss = [], []
        for g in groups:
            st = lax.dot_general(k2, stack(q_s, g), NT, preferred_element_type=f32)
            dp = lax.dot_general(v2, stack(o_s, g), NT, preferred_element_type=f32)
            for u, lh in enumerate(g):
                cs = slice(u * HD, (u + 1) * HD)
                lse = sm_s[qb, lh][None, :] * f32(LOG2E)
                p = jnp.exp2(st[:, cs] * f32(C1) - lse + bias_s[slot])
                ps.append(p.astype(bf))
                dss.append((p * (dp[:, cs] - sm_s[qb, NLH + lh][None, :])).astype(bf))
        pv = jnp.concatenate(ps, axis=1)
        dsv = jnp.concatenate(dss, axis=1)

        def finish():
            dv = lax.dot_general(pv, stack(o_s, everything), NN, preferred_element_type=f32)
            dk = lax.dot_general(dsv, stack(q_s, everything), NN, preferred_element_type=f32)
            acc_s[kb0, :, :HD] += dk[:HD]
            acc_s[kb0, :, HD:] += dv[:HD]
            acc_s[kb1, :, :HD] += dk[HD:]
            acc_s[kb1, :, HD:] += dv[HD:]
            k2t = jnp.concatenate([kT_s[kb0], kT_s[kb1]], axis=1)
            dq_s[qb] += lax.dot_general(k2t, dsv, NN, preferred_element_type=f32)

        return finish

    def trip(r, _):
        last = None
        for slot in range(unroll):
            finish = item(r * unroll + slot, slot)
            if not late:
                finish()
            elif last is not None:
                last()
            last = finish
        if late:
            last()
        return 0

    lax.fori_loop(0, (items + unroll - 1) // unroll, trip, 0)
    scale = f32(HD ** (-0.5))
    dqo_ref[...] = dq_s[0:3] * scale
    dqp_ref[...] = (dq_s[3:6] * scale).astype(bf)
    dkv_ref[:, :, :HD] = (acc_s[:, :, :HD] * scale).astype(bf)
    dkv_ref[:, :, HD:] = acc_s[:, :, HD:].astype(bf)


def attn(ints_o, ints_p, co, small_o, small_p, kv, qo, qp, oo, op, groups=((0, 1), (2, 3), (4, 5), (6, 7), (8,)), unroll=2, late=False, near=False):
    f32 = jnp.float32
    bf = jnp.bfloat16
    smem = pl.BlockSpec(memory_space=pltpu.SMEM)
    vmem = pl.BlockSpec(memory_space=pltpu.VMEM)
    anym = pl.BlockSpec(memory_space=pl.ANY)
    kind = pltpu.VMEM if near else jax.ShapeDtypeStruct
    return pl.pallas_call(
        functools.partial(attn_kernel, groups, unroll, late),
        out_shape=(
            jax.ShapeDtypeStruct((KB, HD, 2 * HD), bf),
            kind((3, HD, NLH * HD), f32),
            kind((3, HD, NLH * HD), bf),
        ),
        in_specs=[smem] * 3 + [vmem] * 3 + [anym] * 4,
        out_specs=(vmem, vmem, vmem),
        scratch_shapes=[
            pltpu.VMEM((2, NL, 384, 384), bf),
            pltpu.VMEM((2, NL, 384, 384), bf),
            pltpu.VMEM((KB, HD, HD), bf),
            pltpu.VMEM((KB, HD, 2 * HD), f32),
            pltpu.VMEM((QB, HD, NLH * HD), f32),
            pltpu.VMEM((QB, 2 * NLH, HD), f32),
            pltpu.VMEM((unroll, 2 * HD, HD), f32),
            pltpu.SMEM((QB * KB + 2 * unroll + 2,), jnp.int32),
            pltpu.SMEM((QB * KB // 2 + unroll + 1,), jnp.int32),
            pltpu.SemaphoreType.DMA((4,)),
        ],
        name="attn",
    )(ints_o, ints_p, co, small_o, small_p, kv, qo, qp, oo, op)


VM = pl.BlockSpec(memory_space=pltpu.VMEM)
SM = pl.BlockSpec(memory_space=pltpu.SMEM)
ANY = pl.BlockSpec(memory_space=pl.ANY)


def kv_kernel(x_ref, w_ref, out_ref, acc_ref):
    step = pl.program_id(0)
    part = jnp.dot(x_ref[...], w_ref[...], preferred_element_type=jnp.float32)

    @pl.when(step == 0)
    def _():
        acc_ref[...] = part

    @pl.when(step > 0)
    def _():
        acc_ref[...] += part

    @pl.when(step == pl.num_programs(0) - 1)
    def _():
        kv = acc_ref[...].astype(jnp.bfloat16)
        for k in range(8):
            out_ref[k] = kv


def project(x, w, steps=2):
    depth = D // steps
    return pl.pallas_call(
        kv_kernel,
        grid=(steps,),
        out_shape=jax.ShapeDtypeStruct((8, 256, 256), jnp.bfloat16),
        in_specs=[
            pl.BlockSpec((256, depth), lambda i: (0, i)),
            pl.BlockSpec((depth, 256), lambda i: (i, 0)),
        ],
        out_specs=pl.BlockSpec((8, 256, 256), lambda i: (0, 0, 0)),
        scratch_shapes=[pltpu.VMEM((256, 256), jnp.float32)],
        name="kv",
    )(x, w)


def sum_kernel(r_ref, out_ref):
    acc = r_ref[0].astype(jnp.float32)
    for k in range(1, 8):
        acc += r_ref[k].astype(jnp.float32)
    out_ref[...] = acc.astype(jnp.bfloat16)


def xt_kernel(co_ref, x_ref, mine_ref, other_ref, flip_ref):
    mine = pl.ds(pl.multiple_of(co_ref[0] * 192, 64), 192)
    other = pl.ds(pl.multiple_of((1 - co_ref[0]) * 192, 64), 192)
    for k in range(8):
        flip_ref[k] = x_ref[:, k * 384 : (k + 1) * 384].T
        mine_ref[k] = flip_ref[k, mine]
        other_ref[k] = flip_ref[k, other]


def split_tokens(co, x):
    part = jax.ShapeDtypeStruct((8, 192, 256), jnp.bfloat16)
    return pl.pallas_call(
        xt_kernel,
        out_shape=(part, part),
        in_specs=[SM, VM],
        out_specs=(VM, VM),
        scratch_shapes=[pltpu.VMEM((8, 384, 256), jnp.bfloat16)],
        name="xt",
    )(co, x)


def dw_kernel(co_ref, xa_ref, xb_ref, ga_ref, gb_ref, out_ref, pair_ref, near_ref, sem):
    pair_ref[co_ref[0]] = ga_ref[...]
    pair_ref[1 - co_ref[0]] = gb_ref[...]
    g = jnp.concatenate([ga_ref[...], gb_ref[...]], axis=0)
    copies = []
    for k in range(8):
        x = jnp.concatenate([xa_ref[k], xb_ref[k]], axis=1)
        near_ref[k] = jnp.dot(x, g, preferred_element_type=jnp.float32).astype(jnp.bfloat16)
        copy = pltpu.make_async_copy(near_ref.at[k], out_ref.at[k], sem.at[k])
        copy.start()
        copies.append(copy)
    for copy in copies:
        copy.wait()


def weight_parts(co, xa, xb, ga, gb):
    return pl.pallas_call(
        dw_kernel,
        out_shape=(
            jax.ShapeDtypeStruct((8, 192, 256), jnp.bfloat16),
            pltpu.VMEM((2, 256, 256), jnp.bfloat16),
        ),
        in_specs=[SM] + [VM] * 4,
        out_specs=(ANY, VM),
        scratch_shapes=[
            pltpu.VMEM((8, 192, 256), jnp.bfloat16),
            pltpu.SemaphoreType.DMA((8,)),
        ],
        compiler_params=pltpu.CompilerParams(vmem_limit_bytes=20 << 20),
        name="dw",
    )(co, xa, xb, ga, gb)


def grad_kernel(r_ref, grad_ref, sq_ref):
    acc = r_ref[0].astype(jnp.float32)
    for k in range(1, 8):
        acc += r_ref[k].astype(jnp.float32)
    grad_ref[...] = acc
    sq = jnp.sum(jnp.sum(acc * acc, axis=0, keepdims=True), axis=1, keepdims=True)
    sq_ref[...] = jnp.broadcast_to(sq, sq_ref.shape)


def scale_kernel(grad_ref, parts_ref, out_ref):
    total = jnp.sum(parts_ref[...], axis=0, keepdims=True)[:, :1]
    out_ref[...] = grad_ref[...] / jnp.sqrt(total / (D * KVH * 2 * HD) + 1e-06)


def dx_kernel(co_ref, g_ref, *refs):
    ra, rb, wa, wb, out_ref = refs[:4], refs[4:8], refs[8:12], refs[12:16], refs[16]

    def total(me, near, far, w_near, w_far):
        acc = lax.dot_general(g_ref[...], w_near[0][...], NT, preferred_element_type=jnp.float32)
        for k in range(4):
            if k > 0:
                acc += lax.dot_general(near[k][me], w_near[k][...], NT, preferred_element_type=jnp.float32)
            acc += lax.dot_general(far[k][me], w_far[k][...], NT, preferred_element_type=jnp.float32)
        out_ref[...] = acc.astype(jnp.bfloat16)

    @pl.when(co_ref[0] == 0)
    def _():
        total(0, ra, rb, wa, wb)

    @pl.when(co_ref[0] == 1)
    def _():
        total(1, rb, ra, wb, wa)


def dq_kernel(a_ref, b_ref, out_ref):
    for b in range(3):
        for lh in range(NLH):
            cs = slice(lh * HD, (lh + 1) * HD)
            t = a_ref[b, :, cs] + b_ref[b, :, cs].astype(jnp.float32)
            h = lh % 3
            out_ref[lh // 3, b * HD : (b + 1) * HD, h * HD : (h + 1) * HD] = t.T.astype(jnp.bfloat16)


def vm(a):
    return pltpu.with_memory_space_constraint(a, pltpu.VMEM)


def call(kernel, specs, *shapes, near=True):
    kind = pltpu.VMEM if near else jax.ShapeDtypeStruct
    out = tuple(kind(s, d) for s, d in shapes)
    return pl.pallas_call(kernel, out_shape=out, in_specs=specs, out_specs=tuple(VM for _ in out))


def swap(a):
    return lax.ppermute(a, "co", [(0, 1), (1, 0)])


def split_shift(a, j):
    perm = []
    for i in range(2):
        for k in range(4):
            if j > 0:
                perm.append((4 * i + k, 4 * i + (k + j) % 4))
            perm.append((8 + 4 * i + k, 8 + 4 * (1 - i) + (k + j) % 4))
    return lax.ppermute(a, ("co", "xh", "z"), perm)


def exchange(a, axes):
    return lax.all_to_all(a, axes, 0, 0)


def step(x_kv, w_kv, queries, d_out, lse, delta, offsets, block_mask):
    f32 = jnp.float32
    bf = jnp.bfloat16
    co = lax.axis_index("co")
    co1 = co.reshape(1).astype(jnp.int32)
    kv_all = exchange(project(x_kv, w_kv), C8)
    xh, z = lax.axis_index("xh"), lax.axis_index("z")
    w_rows = w_kv.reshape(8, 384, 256)
    wa = []
    for j in range(4):
        piece = lax.dynamic_index_in_dim(w_rows, 4 * ((xh + co) % 2) + (z + j) % 4, 0, False)
        got = split_shift(piece, j)
        wa.append(jnp.where(co == 0, piece, got) if j == 0 else got)
    ints = jnp.concatenate([block_mask.reshape(96), offsets, jnp.zeros((31,), jnp.int32)])
    rows = jnp.concatenate([lse, delta], axis=2).reshape(NL, 3, HD, 2, 3)
    small = jnp.transpose(rows, (1, 3, 0, 4, 2)).reshape(3, 2 * NLH, HD)
    xa, xb = split_tokens(co1, x_kv)
    xb = swap(xb)
    dkv, dqo, dqp = attn(
        ints, swap(ints), co1, vm(small), vm(swap(small)),
        vm(kv_all.reshape(KB, HD, 2 * HD)), queries, swap(queries), d_out, swap(d_out),
    )
    dkv_r = exchange(dkv.reshape(8, 256, 256), C8)
    (g,) = call(sum_kernel, [VM], ((256, 256), bf))(vm(dkv_r))
    dw_part, pair = weight_parts(co1, vm(xa), vm(xb), g, vm(swap(g)))
    dw_r = exchange(dw_part, C8)
    grad, sq = call(grad_kernel, [VM], ((192, 256), f32), ((128, HD), f32))(vm(dw_r))
    parts = exchange(sq.reshape(128, 1, HD), ALL)
    ra = [split_shift(pair, j) for j in range(4)]
    rb = [swap(r) for r in ra]
    wb = [swap(w) for w in wa]
    (d_x,) = call(dx_kernel, [SM] + [VM] * 17, ((256, 384), bf), near=False)(
        co1, *map(vm, [g] + ra + rb), *wa, *map(vm, wb)
    )
    (d_queries,) = call(dq_kernel, [VM] * 2, ((NL, 384, 384), bf), near=False)(dqo, vm(swap(dqp)))
    (d_w,) = call(scale_kernel, [VM] * 2, ((192, 256), f32), near=False)(vm(grad), vm(parts.reshape(128, HD)))
    return (d_queries, d_x, d_w)


def solution(mesh):
    mesh5 = Mesh(mesh.devices.reshape(2, 4, 2, 2, 4), ALL)
    ctx = ("xl", "y", "co")
    kvh = ("xh", "z")
    in_specs = (
        P(ctx, None),
        P(None, kvh),
        P(None, ctx, kvh),
        P(None, ctx, kvh),
        P(None, ctx, kvh),
        P(None, ctx, kvh),
        P(ctx),
        P(ctx, None),
    )
    out_specs = (P(None, ctx, kvh), P(ctx, kvh), P(ctx, kvh))
    return jax.shard_map(step, mesh=mesh5, in_specs=in_specs, out_specs=out_specs, check_vma=False)
```

```python
import functools

import jax
import jax.numpy as jnp
from jax import lax
from jax.experimental import pallas as pl
from jax.experimental.pallas import tpu as pltpu
from jax.sharding import Mesh, PartitionSpec as P

D = 3072
KVH = 8
HD = 128
NL = 3
NLH = 9
KB = 16
QB = 6
LOG2E = 1.4426950408889634
C1 = LOG2E * HD ** (-0.5)
NEG = -1e30
NT = (((1,), (1,)), ((), ()))
NN = (((1,), (0,)), ((), ()))
C8 = ("xl", "y")
ALL = ("xl", "y", "co", "xh", "z")


def attn_kernel(groups, unroll, late, ints_o, ints_p, co_ref, small_o, small_p, kv_ref, qo, qp, oo, op, dkv_ref, dqo_ref, dqp_ref,
                q_s, o_s, kT_s, acc_s, dq_s, sm_s, bias_s, dkv_s, dqp_s, lst, one_s, sem, out_sem):
    f32 = jnp.float32
    bf = jnp.bfloat16
    copies = [
        pltpu.make_async_copy(a, d, sem.at[i])
        for i, (a, d) in enumerate(
            [(qo, q_s.at[0]), (oo, o_s.at[0]), (qp, q_s.at[1]), (op, o_s.at[1])]
        )
    ]
    for c in copies:
        c.start()
    co = co_ref[0]
    acc_s[...] = jnp.zeros(acc_s.shape, f32)
    dq_s[...] = jnp.zeros(dq_s.shape, f32)
    sm_s[0:3] = small_o[...]
    sm_s[3:6] = small_p[...]
    for kb in range(KB):
        kT_s[kb] = kv_ref[kb, :, :HD].T

    def key_start(kb):
        j = kb // 2
        return ((j // 4) * 8 + (j % 4) * 2 + co) * 256 + (kb - 2 * j) * 128

    def clear(i, _):
        one_s[i] = jnp.int32(0)
        return 0

    lax.fori_loop(0, one_s.shape[0], clear, 0)
    n = jnp.int32(0)
    for s, ints in ((0, ints_o), (1, ints_p)):
        for b in range(3):
            low = ints[96] + b * 128
            n = n + (n & 1)
            for kb in range(KB):
                j, c = divmod(kb, 2)
                gk = 2 * ((j // 4) * 8 + (j % 4) * 2 + co) + c
                vis = (ints[b * 32 + gk] == 1) & (gk * 128 < low + 127)
                lst[n] = jnp.int32((3 * s + b) * KB + kb)
                n = n + vis.astype(jnp.int32)
            lst[n] = jnp.int32((3 * s + b) * KB)
            one_s[n // 2] = n & 1
    items = (n + 1) // 2
    for extra in range(unroll):
        lst[2 * (items + extra)] = jnp.int32(0)
        lst[2 * (items + extra) + 1] = jnp.int32(0)
        one_s[items + extra] = jnp.int32(2)
    for c in copies:
        c.wait()

    dif = lax.broadcasted_iota(jnp.int32, (HD, HD), 1) - lax.broadcasted_iota(jnp.int32, (HD, HD), 0)
    everything = tuple(range(NLH))

    def item(t, slot):
        code = lst[2 * t]
        qb = code // KB
        kb0 = code - qb * KB
        kb1 = lst[2 * t + 1] - qb * KB
        hide = one_s[t]
        kb1 = jnp.where(hide > 0, kb0, kb1)
        s = qb // 3
        b = qb - 3 * s
        low = jnp.where(s == 0, ints_o[96], ints_p[96]) + b * 128
        far = jnp.int32(1 << 20)
        st0 = jnp.where(hide > 1, far, key_start(kb0)) - low
        st1 = jnp.where(hide > 0, far, key_start(kb1)) - low
        bias_s[slot, 0:HD] = jnp.where(dif > st0, f32(0), f32(NEG))
        bias_s[slot, HD:] = jnp.where(dif > st1, f32(0), f32(NEG))
        rows = pl.ds(pl.multiple_of(b * 128, 128), 128)

        def stack(ref, lhs):
            return jnp.concatenate(
                [ref[s, lh // 3, rows, (lh % 3) * HD : (lh % 3 + 1) * HD] for lh in lhs], axis=0
            )

        k2 = jnp.concatenate([kv_ref[kb0, :, :HD], kv_ref[kb1, :, :HD]], axis=0)
        v2 = jnp.concatenate([kv_ref[kb0, :, HD:], kv_ref[kb1, :, HD:]], axis=0)
        ps, dss = [], []
        for g in groups:
            st = lax.dot_general(k2, stack(q_s, g), NT, preferred_element_type=f32)
            dp = lax.dot_general(v2, stack(o_s, g), NT, preferred_element_type=f32)
            for u, lh in enumerate(g):
                cs = slice(u * HD, (u + 1) * HD)
                lse = sm_s[qb, lh][None, :] * f32(LOG2E)
                p = jnp.exp2(st[:, cs] * f32(C1) - lse + bias_s[slot])
                ps.append(p.astype(bf))
                dss.append((p * (dp[:, cs] - sm_s[qb, NLH + lh][None, :])).astype(bf))
        pv = jnp.concatenate(ps, axis=1)
        dsv = jnp.concatenate(dss, axis=1)

        def finish():
            dv = lax.dot_general(pv, stack(o_s, everything), NN, preferred_element_type=f32)
            dk = lax.dot_general(dsv, stack(q_s, everything), NN, preferred_element_type=f32)
            acc_s[kb0, :, :HD] += dk[:HD]
            acc_s[kb0, :, HD:] += dv[:HD]
            acc_s[kb1, :, :HD] += dk[HD:]
            acc_s[kb1, :, HD:] += dv[HD:]
            k2t = jnp.concatenate([kT_s[kb0], kT_s[kb1]], axis=1)
            dq_s[qb] += lax.dot_general(k2t, dsv, NN, preferred_element_type=f32)

        return finish

    def trip(r, _):
        last = None
        for slot in range(unroll):
            finish = item(r * unroll + slot, slot)
            if not late:
                finish()
            elif last is not None:
                last()
            last = finish
        if late:
            last()
        return 0

    lax.fori_loop(0, (items + unroll - 1) // unroll, trip, 0)
    scale = f32(HD ** (-0.5))

    def send(src, dst, k):
        copy = pltpu.make_async_copy(src, dst, out_sem.at[k])
        copy.start()
        return copy

    sent = [send(dq_s.at[pl.ds(0, 3)], dqo_ref, 0)]
    half = KB // 2
    for k in range(2):
        part = slice(k * half, (k + 1) * half)
        dkv_s[part, :, :HD] = (acc_s[part, :, :HD] * scale).astype(bf)
        dkv_s[part, :, HD:] = acc_s[part, :, HD:].astype(bf)
        sent.append(send(dkv_s.at[pl.ds(k * half, half)], dkv_ref.at[pl.ds(k * half, half)], 1 + k))
    dqp_s[...] = (dq_s[3:6] * scale).astype(bf)
    sent.append(send(dqp_s, dqp_ref, 3))
    for copy in sent:
        copy.wait()


def attn(ints_o, ints_p, co, small_o, small_p, kv, qo, qp, oo, op, groups=((0, 1), (2, 3), (4, 5), (6, 7), (8,)), unroll=4, late=False, near=False):
    f32 = jnp.float32
    bf = jnp.bfloat16
    smem = pl.BlockSpec(memory_space=pltpu.SMEM)
    vmem = pl.BlockSpec(memory_space=pltpu.VMEM)
    anym = pl.BlockSpec(memory_space=pl.ANY)
    kind = pltpu.VMEM if near else jax.ShapeDtypeStruct
    return pl.pallas_call(
        functools.partial(attn_kernel, groups, unroll, late),
        out_shape=(
            jax.ShapeDtypeStruct((KB, HD, 2 * HD), bf),
            kind((3, HD, NLH * HD), f32),
            kind((3, HD, NLH * HD), bf),
        ),
        in_specs=[smem] * 3 + [vmem] * 3 + [anym] * 4,
        out_specs=(anym, anym, anym),
        scratch_shapes=[
            pltpu.VMEM((2, NL, 384, 384), bf),
            pltpu.VMEM((2, NL, 384, 384), bf),
            pltpu.VMEM((KB, HD, HD), bf),
            pltpu.VMEM((KB, HD, 2 * HD), f32),
            pltpu.VMEM((QB, HD, NLH * HD), f32),
            pltpu.VMEM((QB, 2 * NLH, HD), f32),
            pltpu.VMEM((unroll, 2 * HD, HD), f32),
            pltpu.VMEM((KB, HD, 2 * HD), bf),
            pltpu.VMEM((3, HD, NLH * HD), bf),
            pltpu.SMEM((QB * KB + 2 * unroll + 2,), jnp.int32),
            pltpu.SMEM((QB * KB // 2 + unroll + 1,), jnp.int32),
            pltpu.SemaphoreType.DMA((4,)),
            pltpu.SemaphoreType.DMA((4,)),
        ],
        name="attn",
    )(ints_o, ints_p, co, small_o, small_p, kv, qo, qp, oo, op)


VM = pl.BlockSpec(memory_space=pltpu.VMEM)
SM = pl.BlockSpec(memory_space=pltpu.SMEM)
ANY = pl.BlockSpec(memory_space=pl.ANY)


def kv_kernel(x_ref, w_ref, out_ref, acc_ref):
    step = pl.program_id(0)
    part = jnp.dot(x_ref[...], w_ref[...], preferred_element_type=jnp.float32)

    @pl.when(step == 0)
    def _():
        acc_ref[...] = part

    @pl.when(step > 0)
    def _():
        acc_ref[...] += part

    @pl.when(step == pl.num_programs(0) - 1)
    def _():
        kv = acc_ref[...].astype(jnp.bfloat16)
        for k in range(8):
            out_ref[k] = kv


def project(x, w, steps=2):
    depth = D // steps
    return pl.pallas_call(
        kv_kernel,
        grid=(steps,),
        out_shape=jax.ShapeDtypeStruct((8, 256, 256), jnp.bfloat16),
        in_specs=[
            pl.BlockSpec((256, depth), lambda i: (0, i)),
            pl.BlockSpec((depth, 256), lambda i: (i, 0)),
        ],
        out_specs=pl.BlockSpec((8, 256, 256), lambda i: (0, 0, 0)),
        scratch_shapes=[pltpu.VMEM((256, 256), jnp.float32)],
        name="kv",
    )(x, w)


def sum_kernel(r_ref, out_ref):
    acc = r_ref[0].astype(jnp.float32)
    for k in range(1, 8):
        acc += r_ref[k].astype(jnp.float32)
    out_ref[...] = acc.astype(jnp.bfloat16)


def xt_kernel(co_ref, x_ref, mine_ref, other_ref, flip_ref):
    mine = pl.ds(pl.multiple_of(co_ref[0] * 192, 64), 192)
    other = pl.ds(pl.multiple_of((1 - co_ref[0]) * 192, 64), 192)
    for k in range(8):
        flip_ref[k] = x_ref[:, k * 384 : (k + 1) * 384].T
        mine_ref[k] = flip_ref[k, mine]
        other_ref[k] = flip_ref[k, other]


def split_tokens(co, x):
    part = jax.ShapeDtypeStruct((8, 192, 256), jnp.bfloat16)
    return pl.pallas_call(
        xt_kernel,
        out_shape=(part, part),
        in_specs=[SM, VM],
        out_specs=(VM, VM),
        scratch_shapes=[pltpu.VMEM((8, 384, 256), jnp.bfloat16)],
        name="xt",
    )(co, x)


def dw_kernel(co_ref, xa_ref, xb_ref, ga_ref, gb_ref, out_ref, pair_ref, near_ref, sem):
    pair_ref[co_ref[0]] = ga_ref[...]
    pair_ref[1 - co_ref[0]] = gb_ref[...]
    g = jnp.concatenate([ga_ref[...], gb_ref[...]], axis=0)
    copies = []
    for k in range(8):
        x = jnp.concatenate([xa_ref[k], xb_ref[k]], axis=1)
        near_ref[k] = jnp.dot(x, g, preferred_element_type=jnp.float32).astype(jnp.bfloat16)
        copy = pltpu.make_async_copy(near_ref.at[k], out_ref.at[k], sem.at[k])
        copy.start()
        copies.append(copy)
    for copy in copies:
        copy.wait()


def weight_parts(co, xa, xb, ga, gb):
    return pl.pallas_call(
        dw_kernel,
        out_shape=(
            jax.ShapeDtypeStruct((8, 192, 256), jnp.bfloat16),
            pltpu.VMEM((2, 256, 256), jnp.bfloat16),
        ),
        in_specs=[SM] + [VM] * 4,
        out_specs=(ANY, VM),
        scratch_shapes=[
            pltpu.VMEM((8, 192, 256), jnp.bfloat16),
            pltpu.SemaphoreType.DMA((8,)),
        ],
        compiler_params=pltpu.CompilerParams(vmem_limit_bytes=20 << 20),
        name="dw",
    )(co, xa, xb, ga, gb)


def grad_kernel(r_ref, grad_ref, sq_ref):
    acc = r_ref[0].astype(jnp.float32)
    for k in range(1, 8):
        acc += r_ref[k].astype(jnp.float32)
    grad_ref[...] = acc
    sq = jnp.sum(jnp.sum(acc * acc, axis=0, keepdims=True), axis=1, keepdims=True)
    sq_ref[...] = jnp.broadcast_to(sq, sq_ref.shape)


def scale_kernel(grad_ref, parts_ref, out_ref):
    total = jnp.sum(parts_ref[...], axis=0, keepdims=True)[:, :1]
    out_ref[...] = grad_ref[...] / jnp.sqrt(total / (D * KVH * 2 * HD) + 1e-06)


def dx_kernel(co_ref, g_ref, *refs):
    ra, rb, wa, wb, out_ref = refs[:4], refs[4:8], refs[8:12], refs[12:16], refs[16]

    def total(me, near, far, w_near, w_far):
        acc = lax.dot_general(g_ref[...], w_near[0][...], NT, preferred_element_type=jnp.float32)
        for k in range(4):
            if k > 0:
                acc += lax.dot_general(near[k][me], w_near[k][...], NT, preferred_element_type=jnp.float32)
            acc += lax.dot_general(far[k][me], w_far[k][...], NT, preferred_element_type=jnp.float32)
        out_ref[...] = acc.astype(jnp.bfloat16)

    @pl.when(co_ref[0] == 0)
    def _():
        total(0, ra, rb, wa, wb)

    @pl.when(co_ref[0] == 1)
    def _():
        total(1, rb, ra, wb, wa)


def dq_kernel(a_ref, b_ref, out_ref):
    for b in range(3):
        for lh in range(NLH):
            cs = slice(lh * HD, (lh + 1) * HD)
            t = a_ref[b, :, cs] * (HD ** (-0.5)) + b_ref[b, :, cs].astype(jnp.float32)
            h = lh % 3
            out_ref[lh // 3, b * HD : (b + 1) * HD, h * HD : (h + 1) * HD] = t.T.astype(jnp.bfloat16)


def vm(a):
    return pltpu.with_memory_space_constraint(a, pltpu.VMEM)


def call(kernel, specs, *shapes, near=True):
    kind = pltpu.VMEM if near else jax.ShapeDtypeStruct
    out = tuple(kind(s, d) for s, d in shapes)
    return pl.pallas_call(kernel, out_shape=out, in_specs=specs, out_specs=tuple(VM for _ in out))


def swap(a):
    return lax.ppermute(a, "co", [(0, 1), (1, 0)])


def split_shift(a, j):
    perm = []
    for i in range(2):
        for k in range(4):
            if j > 0:
                perm.append((4 * i + k, 4 * i + (k + j) % 4))
            perm.append((8 + 4 * i + k, 8 + 4 * (1 - i) + (k + j) % 4))
    return lax.ppermute(a, ("co", "xh", "z"), perm)


def exchange(a, axes):
    return lax.all_to_all(a, axes, 0, 0)


def step(x_kv, w_kv, queries, d_out, lse, delta, offsets, block_mask):
    f32 = jnp.float32
    bf = jnp.bfloat16
    co = lax.axis_index("co")
    co1 = co.reshape(1).astype(jnp.int32)
    kv_all = exchange(project(x_kv, w_kv), C8)
    xh, z = lax.axis_index("xh"), lax.axis_index("z")
    w_rows = w_kv.reshape(8, 384, 256)
    wa = []
    for j in range(4):
        piece = lax.dynamic_index_in_dim(w_rows, 4 * ((xh + co) % 2) + (z + j) % 4, 0, False)
        got = split_shift(piece, j)
        wa.append(jnp.where(co == 0, piece, got) if j == 0 else got)
    ints = jnp.concatenate([block_mask.reshape(96), offsets, jnp.zeros((31,), jnp.int32)])
    rows = jnp.concatenate([lse, delta], axis=2).reshape(NL, 3, HD, 2, 3)
    small = jnp.transpose(rows, (1, 3, 0, 4, 2)).reshape(3, 2 * NLH, HD)
    xa, xb = split_tokens(co1, x_kv)
    xb = swap(xb)
    dkv, dqo, dqp = attn(
        ints, swap(ints), co1, vm(small), vm(swap(small)),
        vm(kv_all.reshape(KB, HD, 2 * HD)), queries, swap(queries), d_out, swap(d_out),
    )
    dkv_r = exchange(dkv.reshape(8, 256, 256), C8)
    (g,) = call(sum_kernel, [VM], ((256, 256), bf))(vm(dkv_r))
    dw_part, pair = weight_parts(co1, vm(xa), vm(xb), g, vm(swap(g)))
    dw_r = exchange(dw_part, C8)
    grad, sq = call(grad_kernel, [VM], ((192, 256), f32), ((128, HD), f32))(vm(dw_r))
    parts = exchange(sq.reshape(128, 1, HD), ALL)
    ra = [split_shift(pair, j) for j in range(4)]
    rb = [swap(r) for r in ra]
    wb = [swap(w) for w in wa]
    (d_x,) = call(dx_kernel, [SM] + [VM] * 17, ((256, 384), bf), near=False)(
        co1, *map(vm, [g] + ra + rb), *wa, *map(vm, wb)
    )
    (d_queries,) = call(dq_kernel, [VM] * 2, ((NL, 384, 384), bf), near=False)(dqo, vm(swap(dqp)))
    (d_w,) = call(scale_kernel, [VM] * 2, ((192, 256), f32), near=False)(vm(grad), vm(parts.reshape(128, HD)))
    return (d_queries, d_x, d_w)


def solution(mesh):
    mesh5 = Mesh(mesh.devices.reshape(2, 4, 2, 2, 4), ALL)
    ctx = ("xl", "y", "co")
    kvh = ("xh", "z")
    in_specs = (
        P(ctx, None),
        P(None, kvh),
        P(None, ctx, kvh),
        P(None, ctx, kvh),
        P(None, ctx, kvh),
        P(None, ctx, kvh),
        P(ctx),
        P(ctx, None),
    )
    out_specs = (P(None, ctx, kvh), P(ctx, kvh), P(ctx, kvh))
    return jax.shard_map(step, mesh=mesh5, in_specs=in_specs, out_specs=out_specs, check_vma=False)
```

```python
import functools

import jax
import jax.numpy as jnp
from jax import lax
from jax.experimental import pallas as pl
from jax.experimental.pallas import tpu as pltpu
from jax.sharding import Mesh, PartitionSpec as P

D = 3072
KVH = 8
HD = 128
NL = 3
NLH = 9
KB = 16
QB = 6
LOG2E = 1.4426950408889634
C1 = LOG2E * HD ** (-0.5)
NEG = -1e30
NT = (((1,), (1,)), ((), ()))
NN = (((1,), (0,)), ((), ()))
C8 = ("xl", "y")
ALL = ("xl", "y", "co", "xh", "z")


def attn_kernel(groups, unroll, late, ints_o, ints_p, co_ref, small_o, small_p, kv_ref, qo, qp, oo, op, dkv_ref, dqo_ref, dqp_ref,
                q_s, o_s, kT_s, acc_s, dq_s, sm_s, bias_s, dkv_s, dqp_s, lst, one_s, sem, out_sem):
    f32 = jnp.float32
    bf = jnp.bfloat16
    copies = [
        pltpu.make_async_copy(a, d, sem.at[i])
        for i, (a, d) in enumerate(
            [(qo, q_s.at[0]), (oo, o_s.at[0]), (qp, q_s.at[1]), (op, o_s.at[1])]
        )
    ]
    for c in copies:
        c.start()
    co = co_ref[0]
    acc_s[...] = jnp.zeros(acc_s.shape, f32)
    dq_s[...] = jnp.zeros(dq_s.shape, f32)
    sm_s[0:3] = small_o[...]
    sm_s[3:6] = small_p[...]
    for kb in range(KB):
        kT_s[kb] = kv_ref[kb, :, :HD].T

    def key_start(kb):
        j = kb // 2
        return ((j // 4) * 8 + (j % 4) * 2 + co) * 256 + (kb - 2 * j) * 128

    def clear(i, _):
        one_s[i] = jnp.int32(0)
        return 0

    lax.fori_loop(0, one_s.shape[0], clear, 0)
    n = jnp.int32(0)
    for s, ints in ((0, ints_o), (1, ints_p)):
        for b in range(3):
            low = ints[96] + b * 128
            n = n + (n & 1)
            for kb in range(KB):
                j, c = divmod(kb, 2)
                gk = 2 * ((j // 4) * 8 + (j % 4) * 2 + co) + c
                vis = (ints[b * 32 + gk] == 1) & (gk * 128 < low + 127)
                lst[n] = jnp.int32((3 * s + b) * KB + kb)
                n = n + vis.astype(jnp.int32)
            lst[n] = jnp.int32((3 * s + b) * KB)
            one_s[n // 2] = n & 1
    items = (n + 1) // 2
    for extra in range(unroll):
        lst[2 * (items + extra)] = jnp.int32(0)
        lst[2 * (items + extra) + 1] = jnp.int32(0)
        one_s[items + extra] = jnp.int32(2)
    for c in copies:
        c.wait()

    dif = lax.broadcasted_iota(jnp.int32, (HD, HD), 1) - lax.broadcasted_iota(jnp.int32, (HD, HD), 0)
    everything = tuple(range(NLH))

    def item(t, slot):
        code = lst[2 * t]
        qb = code // KB
        kb0 = code - qb * KB
        kb1 = lst[2 * t + 1] - qb * KB
        hide = one_s[t]
        kb1 = jnp.where(hide > 0, kb0, kb1)
        s = qb // 3
        b = qb - 3 * s
        low = jnp.where(s == 0, ints_o[96], ints_p[96]) + b * 128
        far = jnp.int32(1 << 20)
        st0 = jnp.where(hide > 1, far, key_start(kb0)) - low
        st1 = jnp.where(hide > 0, far, key_start(kb1)) - low
        bias_s[slot, 0:HD] = jnp.where(dif > st0, f32(0), f32(NEG))
        bias_s[slot, HD:] = jnp.where(dif > st1, f32(0), f32(NEG))
        rows = pl.ds(pl.multiple_of(b * 128, 128), 128)

        def stack(ref, lhs):
            return jnp.concatenate(
                [ref[s, lh // 3, rows, (lh % 3) * HD : (lh % 3 + 1) * HD] for lh in lhs], axis=0
            )

        k2 = jnp.concatenate([kv_ref[kb0, :, :HD], kv_ref[kb1, :, :HD]], axis=0)
        v2 = jnp.concatenate([kv_ref[kb0, :, HD:], kv_ref[kb1, :, HD:]], axis=0)
        ps, dss = [], []
        for g in groups:
            st = lax.dot_general(k2, stack(q_s, g), NT, preferred_element_type=f32)
            dp = lax.dot_general(v2, stack(o_s, g), NT, preferred_element_type=f32)
            for u, lh in enumerate(g):
                cs = slice(u * HD, (u + 1) * HD)
                lse = sm_s[qb, lh][None, :] * f32(LOG2E)
                p = jnp.exp2(st[:, cs] * f32(C1) - lse + bias_s[slot])
                ps.append(p.astype(bf))
                dss.append((p * (dp[:, cs] - sm_s[qb, NLH + lh][None, :])).astype(bf))
        pv = jnp.concatenate(ps, axis=1)
        dsv = jnp.concatenate(dss, axis=1)

        def finish():
            dv = lax.dot_general(pv, stack(o_s, everything), NN, preferred_element_type=f32)
            dk = lax.dot_general(dsv, stack(q_s, everything), NN, preferred_element_type=f32)
            acc_s[kb0, :, :HD] += dk[:HD]
            acc_s[kb0, :, HD:] += dv[:HD]
            acc_s[kb1, :, :HD] += dk[HD:]
            acc_s[kb1, :, HD:] += dv[HD:]
            k2t = jnp.concatenate([kT_s[kb0], kT_s[kb1]], axis=1)
            dq_s[qb] += lax.dot_general(k2t, dsv, NN, preferred_element_type=f32)

        return finish

    def trip(r, _):
        last = None
        for slot in range(unroll):
            finish = item(r * unroll + slot, slot)
            if not late:
                finish()
            elif last is not None:
                last()
            last = finish
        if late:
            last()
        return 0

    lax.fori_loop(0, (items + unroll - 1) // unroll, trip, 0)
    scale = f32(HD ** (-0.5))

    def send(src, dst, k):
        copy = pltpu.make_async_copy(src, dst, out_sem.at[k])
        copy.start()
        return copy

    sent = [send(dq_s.at[pl.ds(0, 3)], dqo_ref, 0)]
    half = KB // 2
    for k in range(2):
        part = slice(k * half, (k + 1) * half)
        dkv_s[part, :, :HD] = (acc_s[part, :, :HD] * scale).astype(bf)
        dkv_s[part, :, HD:] = acc_s[part, :, HD:].astype(bf)
        sent.append(send(dkv_s.at[pl.ds(k * half, half)], dkv_ref.at[pl.ds(k * half, half)], 1 + k))
    dqp_s[...] = (dq_s[3:6] * scale).astype(bf)
    sent.append(send(dqp_s, dqp_ref, 3))
    for copy in sent:
        copy.wait()


def attn(ints_o, ints_p, co, small_o, small_p, kv, qo, qp, oo, op, groups=((0, 1), (2, 3), (4, 5), (6, 7), (8,)), unroll=4, late=False, near=False):
    f32 = jnp.float32
    bf = jnp.bfloat16
    smem = pl.BlockSpec(memory_space=pltpu.SMEM)
    vmem = pl.BlockSpec(memory_space=pltpu.VMEM)
    anym = pl.BlockSpec(memory_space=pl.ANY)
    kind = pltpu.VMEM if near else jax.ShapeDtypeStruct
    return pl.pallas_call(
        functools.partial(attn_kernel, groups, unroll, late),
        out_shape=(
            jax.ShapeDtypeStruct((KB, HD, 2 * HD), bf),
            kind((3, HD, NLH * HD), f32),
            kind((3, HD, NLH * HD), bf),
        ),
        in_specs=[smem] * 3 + [vmem] * 3 + [anym] * 4,
        out_specs=(anym, anym, anym),
        scratch_shapes=[
            pltpu.VMEM((2, NL, 384, 384), bf),
            pltpu.VMEM((2, NL, 384, 384), bf),
            pltpu.VMEM((KB, HD, HD), bf),
            pltpu.VMEM((KB, HD, 2 * HD), f32),
            pltpu.VMEM((QB, HD, NLH * HD), f32),
            pltpu.VMEM((QB, 2 * NLH, HD), f32),
            pltpu.VMEM((unroll, 2 * HD, HD), f32),
            pltpu.VMEM((KB, HD, 2 * HD), bf),
            pltpu.VMEM((3, HD, NLH * HD), bf),
            pltpu.SMEM((QB * KB + 2 * unroll + 2,), jnp.int32),
            pltpu.SMEM((QB * KB // 2 + unroll + 1,), jnp.int32),
            pltpu.SemaphoreType.DMA((4,)),
            pltpu.SemaphoreType.DMA((4,)),
        ],
        name="attn",
    )(ints_o, ints_p, co, small_o, small_p, kv, qo, qp, oo, op)


VM = pl.BlockSpec(memory_space=pltpu.VMEM)
SM = pl.BlockSpec(memory_space=pltpu.SMEM)
ANY = pl.BlockSpec(memory_space=pl.ANY)


def kv_kernel(x_ref, w_ref, out_ref, acc_ref):
    step = pl.program_id(0)
    part = jnp.dot(x_ref[...], w_ref[...], preferred_element_type=jnp.float32)

    @pl.when(step == 0)
    def _():
        acc_ref[...] = part

    @pl.when(step > 0)
    def _():
        acc_ref[...] += part

    @pl.when(step == pl.num_programs(0) - 1)
    def _():
        kv = acc_ref[...].astype(jnp.bfloat16)
        for k in range(8):
            out_ref[k] = kv


def project(x, w, steps=2):
    depth = D // steps
    return pl.pallas_call(
        kv_kernel,
        grid=(steps,),
        out_shape=jax.ShapeDtypeStruct((8, 256, 256), jnp.bfloat16),
        in_specs=[
            pl.BlockSpec((256, depth), lambda i: (0, i)),
            pl.BlockSpec((depth, 256), lambda i: (i, 0)),
        ],
        out_specs=pl.BlockSpec((8, 256, 256), lambda i: (0, 0, 0)),
        scratch_shapes=[pltpu.VMEM((256, 256), jnp.float32)],
        name="kv",
    )(x, w)


def sum_kernel(r_ref, out_ref):
    acc = r_ref[0].astype(jnp.float32)
    for k in range(1, 8):
        acc += r_ref[k].astype(jnp.float32)
    out_ref[...] = acc.astype(jnp.bfloat16)


def xt_kernel(co_ref, x_ref, mine_ref, other_ref, flip_ref):
    mine = pl.ds(pl.multiple_of(co_ref[0] * 192, 64), 192)
    other = pl.ds(pl.multiple_of((1 - co_ref[0]) * 192, 64), 192)
    for k in range(8):
        flip_ref[k] = x_ref[:, k * 384 : (k + 1) * 384].T
        mine_ref[k] = flip_ref[k, mine]
        other_ref[k] = flip_ref[k, other]


def split_tokens(co, x):
    part = jax.ShapeDtypeStruct((8, 192, 256), jnp.bfloat16)
    return pl.pallas_call(
        xt_kernel,
        out_shape=(part, part),
        in_specs=[SM, VM],
        out_specs=(VM, VM),
        scratch_shapes=[pltpu.VMEM((8, 384, 256), jnp.bfloat16)],
        name="xt",
    )(co, x)


def dw_kernel(co_ref, xa_ref, xb_ref, ga_ref, gb_ref, out_ref, pair_ref, near_ref, sem):
    pair_ref[co_ref[0]] = ga_ref[...]
    pair_ref[1 - co_ref[0]] = gb_ref[...]
    g = jnp.concatenate([ga_ref[...], gb_ref[...]], axis=0)
    copies = []
    for k in range(8):
        x = jnp.concatenate([xa_ref[k], xb_ref[k]], axis=1)
        near_ref[k] = jnp.dot(x, g, preferred_element_type=jnp.float32).astype(jnp.bfloat16)
        copy = pltpu.make_async_copy(near_ref.at[k], out_ref.at[k], sem.at[k])
        copy.start()
        copies.append(copy)
    for copy in copies:
        copy.wait()


def weight_parts(co, xa, xb, ga, gb):
    return pl.pallas_call(
        dw_kernel,
        out_shape=(
            jax.ShapeDtypeStruct((8, 192, 256), jnp.bfloat16),
            pltpu.VMEM((2, 256, 256), jnp.bfloat16),
        ),
        in_specs=[SM] + [VM] * 4,
        out_specs=(ANY, VM),
        scratch_shapes=[
            pltpu.VMEM((8, 192, 256), jnp.bfloat16),
            pltpu.SemaphoreType.DMA((8,)),
        ],
        compiler_params=pltpu.CompilerParams(vmem_limit_bytes=20 << 20),
        name="dw",
    )(co, xa, xb, ga, gb)


def grad_kernel(r_ref, grad_ref, sq_ref):
    acc = r_ref[0].astype(jnp.float32)
    for k in range(1, 8):
        acc += r_ref[k].astype(jnp.float32)
    grad_ref[...] = acc
    sq = jnp.sum(jnp.sum(acc * acc, axis=0, keepdims=True), axis=1, keepdims=True)
    sq_ref[...] = jnp.broadcast_to(sq, sq_ref.shape)


def scale_kernel(grad_ref, parts_ref, out_ref):
    total = jnp.sum(parts_ref[...], axis=0, keepdims=True)[:, :1]
    out_ref[...] = grad_ref[...] / jnp.sqrt(total / (D * KVH * 2 * HD) + 1e-06)


def dx_kernel(co_ref, g_ref, w_ref, *refs):
    ra, rb, wa, wb, out_ref = refs[:4], refs[4:8], refs[8:12], refs[12:16], refs[16]

    def total(me, near, far, w_near, w_far):
        acc = lax.dot_general(g_ref[...], w_ref[...], NT, preferred_element_type=jnp.float32)
        for k in range(4):
            if k > 0:
                acc += lax.dot_general(near[k][me], w_near[k][...], NT, preferred_element_type=jnp.float32)
            acc += lax.dot_general(far[k][me], w_far[k][...], NT, preferred_element_type=jnp.float32)
        out_ref[...] = acc.astype(jnp.bfloat16)

    @pl.when(co_ref[0] == 0)
    def _():
        total(0, ra, rb, wa, wb)

    @pl.when(co_ref[0] == 1)
    def _():
        total(1, rb, ra, wb, wa)


def dq_kernel(a_ref, b_ref, out_ref):
    for b in range(3):
        for lh in range(NLH):
            cs = slice(lh * HD, (lh + 1) * HD)
            t = a_ref[b, :, cs] * (HD ** (-0.5)) + b_ref[b, :, cs].astype(jnp.float32)
            h = lh % 3
            out_ref[lh // 3, b * HD : (b + 1) * HD, h * HD : (h + 1) * HD] = t.T.astype(jnp.bfloat16)


def vm(a):
    return pltpu.with_memory_space_constraint(a, pltpu.VMEM)


def call(kernel, specs, *shapes, near=True):
    kind = pltpu.VMEM if near else jax.ShapeDtypeStruct
    out = tuple(kind(s, d) for s, d in shapes)
    return pl.pallas_call(kernel, out_shape=out, in_specs=specs, out_specs=tuple(VM for _ in out))


def swap(a):
    return lax.ppermute(a, "co", [(0, 1), (1, 0)])


def split_shift(a, j):
    perm = []
    for i in range(2):
        for k in range(4):
            if j > 0:
                perm.append((4 * i + k, 4 * i + (k + j) % 4))
            perm.append((8 + 4 * i + k, 8 + 4 * (1 - i) + (k + j) % 4))
    return lax.ppermute(a, ("co", "xh", "z"), perm)


def exchange(a, axes):
    return lax.all_to_all(a, axes, 0, 0)


def step(x_kv, w_kv, queries, d_out, lse, delta, offsets, block_mask):
    f32 = jnp.float32
    bf = jnp.bfloat16
    co = lax.axis_index("co")
    co1 = co.reshape(1).astype(jnp.int32)
    kv_all = exchange(project(x_kv, w_kv), C8)
    xh, z = lax.axis_index("xh"), lax.axis_index("z")
    w_rows = w_kv.reshape(8, 384, 256)
    wa = []
    for j in range(4):
        piece = lax.dynamic_index_in_dim(w_rows, 4 * ((xh + co) % 2) + (z + j) % 4, 0, False)
        wa.append(split_shift(piece, j))
    w_own = lax.dynamic_index_in_dim(w_rows, 4 * xh + z, 0, False)
    ints = jnp.concatenate([block_mask.reshape(96), offsets, jnp.zeros((31,), jnp.int32)])
    rows = jnp.concatenate([lse, delta], axis=2).reshape(NL, 3, HD, 2, 3)
    small = jnp.transpose(rows, (1, 3, 0, 4, 2)).reshape(3, 2 * NLH, HD)
    xa, xb = split_tokens(co1, x_kv)
    xb = swap(xb)
    dkv, dqo, dqp = attn(
        ints, swap(ints), co1, vm(small), vm(swap(small)),
        vm(kv_all.reshape(KB, HD, 2 * HD)), queries, swap(queries), d_out, swap(d_out),
    )
    dkv_r = exchange(dkv.reshape(8, 256, 256), C8)
    (g,) = call(sum_kernel, [VM], ((256, 256), bf))(vm(dkv_r))
    dw_part, pair = weight_parts(co1, vm(xa), vm(xb), g, vm(swap(g)))
    dw_r = exchange(dw_part, C8)
    grad, sq = call(grad_kernel, [VM], ((192, 256), f32), ((128, HD), f32))(vm(dw_r))
    parts = exchange(sq.reshape(128, 1, HD), ALL)
    ra = [split_shift(pair, j) for j in range(4)]
    rb = [swap(r) for r in ra]
    wb = [swap(w) for w in wa]
    (d_x,) = call(dx_kernel, [SM] + [VM] * 18, ((256, 384), bf), near=False)(
        co1, vm(g), w_own, *map(vm, ra + rb), *wa, *map(vm, wb)
    )
    (d_queries,) = call(dq_kernel, [VM] * 2, ((NL, 384, 384), bf), near=False)(dqo, vm(swap(dqp)))
    (d_w,) = call(scale_kernel, [VM] * 2, ((192, 256), f32), near=False)(vm(grad), vm(parts.reshape(128, HD)))
    return (d_queries, d_x, d_w)


def solution(mesh):
    mesh5 = Mesh(mesh.devices.reshape(2, 4, 2, 2, 4), ALL)
    ctx = ("xl", "y", "co")
    kvh = ("xh", "z")
    in_specs = (
        P(ctx, None),
        P(None, kvh),
        P(None, ctx, kvh),
        P(None, ctx, kvh),
        P(None, ctx, kvh),
        P(None, ctx, kvh),
        P(ctx),
        P(ctx, None),
    )
    out_specs = (P(None, ctx, kvh), P(ctx, kvh), P(ctx, kvh))
    return jax.shard_map(step, mesh=mesh5, in_specs=in_specs, out_specs=out_specs, check_vma=False)
```

```python
import functools

import jax
import jax.numpy as jnp
from jax import lax
from jax.experimental import pallas as pl
from jax.experimental.pallas import tpu as pltpu
from jax.sharding import Mesh, PartitionSpec as P

D = 3072
KVH = 8
HD = 128
NL = 3
NLH = 9
KB = 16
QB = 6
LOG2E = 1.4426950408889634
C1 = LOG2E * HD ** (-0.5)
NEG = -1e30
NT = (((1,), (1,)), ((), ()))
NN = (((1,), (0,)), ((), ()))
C8 = ("xl", "y")
ALL = ("xl", "y", "co", "xh", "z")


def attn_kernel(groups, unroll, late, ints_o, ints_p, co_ref, small_o, small_p, kv_ref, qo, qp, oo, op, dkv_ref, dqo_ref, dqp_ref,
                q_s, o_s, kT_s, acc_s, dq_s, sm_s, bias_s, dkv_s, dqp_s, lst, one_s, sem, out_sem):
    f32 = jnp.float32
    bf = jnp.bfloat16
    copies = [
        pltpu.make_async_copy(a, d, sem.at[i])
        for i, (a, d) in enumerate(
            [(qo, q_s.at[0]), (oo, o_s.at[0]), (qp, q_s.at[1]), (op, o_s.at[1])]
        )
    ]
    for c in copies:
        c.start()
    co = co_ref[0]
    acc_s[...] = jnp.zeros(acc_s.shape, f32)
    dq_s[...] = jnp.zeros(dq_s.shape, f32)
    sm_s[0:3] = small_o[...]
    sm_s[3:6] = small_p[...]
    for kb in range(KB):
        kT_s[kb] = kv_ref[kb, :, :HD].T

    def key_start(kb):
        j = kb // 2
        return ((j // 4) * 8 + (j % 4) * 2 + co) * 256 + (kb - 2 * j) * 128

    def clear(i, _):
        one_s[i] = jnp.int32(0)
        return 0

    lax.fori_loop(0, one_s.shape[0], clear, 0)
    n = jnp.int32(0)
    for s, ints in ((0, ints_o), (1, ints_p)):
        for b in range(3):
            low = ints[96] + b * 128
            n = n + (n & 1)
            for kb in range(KB):
                j, c = divmod(kb, 2)
                gk = 2 * ((j // 4) * 8 + (j % 4) * 2 + co) + c
                vis = (ints[b * 32 + gk] == 1) & (gk * 128 < low + 127)
                lst[n] = jnp.int32((3 * s + b) * KB + kb)
                n = n + vis.astype(jnp.int32)
            lst[n] = jnp.int32((3 * s + b) * KB)
            one_s[n // 2] = n & 1
    items = (n + 1) // 2
    for extra in range(unroll):
        lst[2 * (items + extra)] = jnp.int32(0)
        lst[2 * (items + extra) + 1] = jnp.int32(0)
        one_s[items + extra] = jnp.int32(2)
    for c in copies:
        c.wait()

    dif = lax.broadcasted_iota(jnp.int32, (HD, HD), 1) - lax.broadcasted_iota(jnp.int32, (HD, HD), 0)
    everything = tuple(range(NLH))

    def item(t, slot):
        code = lst[2 * t]
        qb = code // KB
        kb0 = code - qb * KB
        kb1 = lst[2 * t + 1] - qb * KB
        hide = one_s[t]
        kb1 = jnp.where(hide > 0, kb0, kb1)
        s = qb // 3
        b = qb - 3 * s
        low = jnp.where(s == 0, ints_o[96], ints_p[96]) + b * 128
        far = jnp.int32(1 << 20)
        st0 = jnp.where(hide > 1, far, key_start(kb0)) - low
        st1 = jnp.where(hide > 0, far, key_start(kb1)) - low
        bias_s[slot, 0:HD] = jnp.where(dif > st0, f32(0), f32(NEG))
        bias_s[slot, HD:] = jnp.where(dif > st1, f32(0), f32(NEG))
        rows = pl.ds(pl.multiple_of(b * 128, 128), 128)

        def stack(ref, lhs):
            return jnp.concatenate(
                [ref[s, lh // 3, rows, (lh % 3) * HD : (lh % 3 + 1) * HD] for lh in lhs], axis=0
            )

        k2 = jnp.concatenate([kv_ref[kb0, :, :HD], kv_ref[kb1, :, :HD]], axis=0)
        v2 = jnp.concatenate([kv_ref[kb0, :, HD:], kv_ref[kb1, :, HD:]], axis=0)
        ps, dss = [], []
        for g in groups:
            st = lax.dot_general(k2, stack(q_s, g), NT, preferred_element_type=f32)
            dp = lax.dot_general(v2, stack(o_s, g), NT, preferred_element_type=f32)
            for u, lh in enumerate(g):
                cs = slice(u * HD, (u + 1) * HD)
                lse = sm_s[qb, lh][None, :] * f32(LOG2E)
                p = jnp.exp2(st[:, cs] * f32(C1) - lse + bias_s[slot])
                ps.append(p.astype(bf))
                dss.append((p * (dp[:, cs] - sm_s[qb, NLH + lh][None, :])).astype(bf))
        pv = jnp.concatenate(ps, axis=1)
        dsv = jnp.concatenate(dss, axis=1)

        def finish():
            dv = lax.dot_general(pv, stack(o_s, everything), NN, preferred_element_type=f32)
            dk = lax.dot_general(dsv, stack(q_s, everything), NN, preferred_element_type=f32)
            acc_s[kb0, :, :HD] += dk[:HD]
            acc_s[kb0, :, HD:] += dv[:HD]
            acc_s[kb1, :, :HD] += dk[HD:]
            acc_s[kb1, :, HD:] += dv[HD:]
            k2t = jnp.concatenate([kT_s[kb0], kT_s[kb1]], axis=1)
            dq_s[qb] += lax.dot_general(k2t, dsv, NN, preferred_element_type=f32)

        return finish

    def trip(r, _):
        last = None
        for slot in range(unroll):
            finish = item(r * unroll + slot, slot)
            if not late:
                finish()
            elif last is not None:
                last()
            last = finish
        if late:
            last()
        return 0

    lax.fori_loop(0, (items + unroll - 1) // unroll, trip, 0)
    scale = f32(HD ** (-0.5))

    def send(src, dst, k):
        copy = pltpu.make_async_copy(src, dst, out_sem.at[k])
        copy.start()
        return copy

    sent = [send(dq_s.at[pl.ds(0, 3)], dqo_ref, 0)]
    half = KB // 2
    for k in range(2):
        part = slice(k * half, (k + 1) * half)
        dkv_s[part, :, :HD] = (acc_s[part, :, :HD] * scale).astype(bf)
        dkv_s[part, :, HD:] = acc_s[part, :, HD:].astype(bf)
        sent.append(send(dkv_s.at[pl.ds(k * half, half)], dkv_ref.at[pl.ds(k * half, half)], 1 + k))
    dqp_s[...] = (dq_s[3:6] * scale).astype(bf)
    sent.append(send(dqp_s, dqp_ref, 3))
    for copy in sent:
        copy.wait()


def attn(ints_o, ints_p, co, small_o, small_p, kv, qo, qp, oo, op, groups=((0, 1), (2, 3), (4, 5), (6, 7), (8,)), unroll=4, late=False, near=False):
    f32 = jnp.float32
    bf = jnp.bfloat16
    smem = pl.BlockSpec(memory_space=pltpu.SMEM)
    vmem = pl.BlockSpec(memory_space=pltpu.VMEM)
    anym = pl.BlockSpec(memory_space=pl.ANY)
    kind = pltpu.VMEM if near else jax.ShapeDtypeStruct
    return pl.pallas_call(
        functools.partial(attn_kernel, groups, unroll, late),
        out_shape=(
            jax.ShapeDtypeStruct((KB, HD, 2 * HD), bf),
            kind((3, HD, NLH * HD), f32),
            kind((3, HD, NLH * HD), bf),
        ),
        in_specs=[smem] * 3 + [vmem] * 3 + [anym] * 4,
        out_specs=(anym, anym, anym),
        scratch_shapes=[
            pltpu.VMEM((2, NL, 384, 384), bf),
            pltpu.VMEM((2, NL, 384, 384), bf),
            pltpu.VMEM((KB, HD, HD), bf),
            pltpu.VMEM((KB, HD, 2 * HD), f32),
            pltpu.VMEM((QB, HD, NLH * HD), f32),
            pltpu.VMEM((QB, 2 * NLH, HD), f32),
            pltpu.VMEM((unroll, 2 * HD, HD), f32),
            pltpu.VMEM((KB, HD, 2 * HD), bf),
            pltpu.VMEM((3, HD, NLH * HD), bf),
            pltpu.SMEM((QB * KB + 2 * unroll + 2,), jnp.int32),
            pltpu.SMEM((QB * KB // 2 + unroll + 1,), jnp.int32),
            pltpu.SemaphoreType.DMA((4,)),
            pltpu.SemaphoreType.DMA((4,)),
        ],
        name="attn",
    )(ints_o, ints_p, co, small_o, small_p, kv, qo, qp, oo, op)


VM = pl.BlockSpec(memory_space=pltpu.VMEM)
SM = pl.BlockSpec(memory_space=pltpu.SMEM)
ANY = pl.BlockSpec(memory_space=pl.ANY)


def kv_kernel(x_ref, w_ref, out_ref, acc_ref):
    step = pl.program_id(0)
    part = jnp.dot(x_ref[...], w_ref[...], preferred_element_type=jnp.float32)

    @pl.when(step == 0)
    def _():
        acc_ref[...] = part

    @pl.when(step > 0)
    def _():
        acc_ref[...] += part

    @pl.when(step == pl.num_programs(0) - 1)
    def _():
        kv = acc_ref[...].astype(jnp.bfloat16)
        for k in range(8):
            out_ref[k] = kv


def project(x, w, steps=2):
    depth = D // steps
    return pl.pallas_call(
        kv_kernel,
        grid=(steps,),
        out_shape=jax.ShapeDtypeStruct((8, 256, 256), jnp.bfloat16),
        in_specs=[
            pl.BlockSpec((256, depth), lambda i: (0, i)),
            pl.BlockSpec((depth, 256), lambda i: (i, 0)),
        ],
        out_specs=pl.BlockSpec((8, 256, 256), lambda i: (0, 0, 0)),
        scratch_shapes=[pltpu.VMEM((256, 256), jnp.float32)],
        name="kv",
    )(x, w)


def sum_kernel(r_ref, out_ref):
    acc = r_ref[0].astype(jnp.float32)
    for k in range(1, 8):
        acc += r_ref[k].astype(jnp.float32)
    out_ref[...] = acc.astype(jnp.bfloat16)


def xt_kernel(co_ref, x_ref, mine_ref, other_ref, flip_ref):
    mine = pl.ds(pl.multiple_of(co_ref[0] * 192, 64), 192)
    other = pl.ds(pl.multiple_of((1 - co_ref[0]) * 192, 64), 192)
    for k in range(8):
        flip_ref[k] = x_ref[:, k * 384 : (k + 1) * 384].T
        mine_ref[k] = flip_ref[k, mine]
        other_ref[k] = flip_ref[k, other]


def split_tokens(co, x):
    part = jax.ShapeDtypeStruct((8, 192, 256), jnp.bfloat16)
    return pl.pallas_call(
        xt_kernel,
        out_shape=(part, part),
        in_specs=[SM, VM],
        out_specs=(VM, VM),
        scratch_shapes=[pltpu.VMEM((8, 384, 256), jnp.bfloat16)],
        name="xt",
    )(co, x)


def dw_kernel(co_ref, xa_ref, xb_ref, ga_ref, gb_ref, out_ref, pair_ref, near_ref, sem):
    pair_ref[co_ref[0]] = ga_ref[...]
    pair_ref[1 - co_ref[0]] = gb_ref[...]
    g = jnp.concatenate([ga_ref[...], gb_ref[...]], axis=0)
    copies = []
    for k in range(8):
        x = jnp.concatenate([xa_ref[k], xb_ref[k]], axis=1)
        near_ref[k] = jnp.dot(x, g, preferred_element_type=jnp.float32).astype(jnp.bfloat16)
        copy = pltpu.make_async_copy(near_ref.at[k], out_ref.at[k], sem.at[k])
        copy.start()
        copies.append(copy)
    for copy in copies:
        copy.wait()


def weight_parts(co, xa, xb, ga, gb):
    return pl.pallas_call(
        dw_kernel,
        out_shape=(
            jax.ShapeDtypeStruct((8, 192, 256), jnp.bfloat16),
            pltpu.VMEM((2, 256, 256), jnp.bfloat16),
        ),
        in_specs=[SM] + [VM] * 4,
        out_specs=(ANY, VM),
        scratch_shapes=[
            pltpu.VMEM((8, 192, 256), jnp.bfloat16),
            pltpu.SemaphoreType.DMA((8,)),
        ],
        compiler_params=pltpu.CompilerParams(vmem_limit_bytes=20 << 20),
        name="dw",
    )(co, xa, xb, ga, gb)


def grad_kernel(r_ref, grad_ref, sq_ref):
    acc = r_ref[0].astype(jnp.float32)
    for k in range(1, 8):
        acc += r_ref[k].astype(jnp.float32)
    grad_ref[...] = acc
    sq = jnp.sum(jnp.sum(acc * acc, axis=0, keepdims=True), axis=1, keepdims=True)
    sq_ref[...] = jnp.broadcast_to(sq, sq_ref.shape)


def scale_kernel(grad_ref, parts_ref, out_ref):
    total = jnp.sum(parts_ref[...], axis=0, keepdims=True)[:, :1]
    out_ref[...] = grad_ref[...] / jnp.sqrt(total / (D * KVH * 2 * HD) + 1e-06)


def dx_kernel(co_ref, g_ref, *refs):
    ra, rb, wb, far = refs[:4], refs[4:8], refs[8:12], refs[12:17]
    out_ref, w_s, acc_s, sem = refs[17:]
    copies = [pltpu.make_async_copy(w, w_s.at[k], sem.at[k]) for k, w in enumerate(far)]
    for copy in copies:
        copy.start()

    def add(acc, me, skip, grads, weights):
        for k in range(skip, 4):
            acc += lax.dot_general(grads[k][me], weights(k), NT, preferred_element_type=jnp.float32)
        return acc

    for me in range(2):
        @pl.when(co_ref[0] == me)
        def _():
            zero = jnp.zeros((256, 384), jnp.float32)
            acc_s[...] = add(zero, me, me, rb, lambda k: wb[k][...])

    for copy in copies:
        copy.wait()
    for me in range(2):
        @pl.when(co_ref[0] == me)
        def _():
            acc = acc_s[...] + lax.dot_general(
                g_ref[...], w_s[4], NT, preferred_element_type=jnp.float32
            )
            out_ref[...] = add(acc, me, 1 - me, ra, lambda k: w_s[k]).astype(jnp.bfloat16)


def input_grads(co, g, ra, rb, wb, wa, w_own):
    return pl.pallas_call(
        dx_kernel,
        out_shape=jax.ShapeDtypeStruct((256, 384), jnp.bfloat16),
        in_specs=[SM] + [VM] * 13 + [ANY] * 5,
        out_specs=VM,
        scratch_shapes=[
            pltpu.VMEM((5, 384, 256), jnp.bfloat16),
            pltpu.VMEM((256, 384), jnp.float32),
            pltpu.SemaphoreType.DMA((5,)),
        ],
        compiler_params=pltpu.CompilerParams(vmem_limit_bytes=20 << 20),
        name="dx",
    )(co, *map(vm, [g] + ra + rb + wb), *wa, w_own)


def dq_kernel(a_ref, b_ref, out_ref):
    for b in range(3):
        for lh in range(NLH):
            cs = slice(lh * HD, (lh + 1) * HD)
            t = a_ref[b, :, cs] * (HD ** (-0.5)) + b_ref[b, :, cs].astype(jnp.float32)
            h = lh % 3
            out_ref[lh // 3, b * HD : (b + 1) * HD, h * HD : (h + 1) * HD] = t.T.astype(jnp.bfloat16)


def vm(a):
    return pltpu.with_memory_space_constraint(a, pltpu.VMEM)


def call(kernel, specs, *shapes, near=True):
    kind = pltpu.VMEM if near else jax.ShapeDtypeStruct
    out = tuple(kind(s, d) for s, d in shapes)
    return pl.pallas_call(kernel, out_shape=out, in_specs=specs, out_specs=tuple(VM for _ in out))


def swap(a):
    return lax.ppermute(a, "co", [(0, 1), (1, 0)])


def split_shift(a, j):
    perm = []
    for i in range(2):
        for k in range(4):
            if j > 0:
                perm.append((4 * i + k, 4 * i + (k + j) % 4))
            perm.append((8 + 4 * i + k, 8 + 4 * (1 - i) + (k + j) % 4))
    return lax.ppermute(a, ("co", "xh", "z"), perm)


def exchange(a, axes):
    return lax.all_to_all(a, axes, 0, 0)


def step(x_kv, w_kv, queries, d_out, lse, delta, offsets, block_mask):
    f32 = jnp.float32
    bf = jnp.bfloat16
    co = lax.axis_index("co")
    co1 = co.reshape(1).astype(jnp.int32)
    kv_all = exchange(project(x_kv, w_kv), C8)
    xh, z = lax.axis_index("xh"), lax.axis_index("z")
    w_rows = w_kv.reshape(8, 384, 256)
    wa = []
    for j in range(4):
        piece = lax.dynamic_index_in_dim(w_rows, 4 * ((xh + co) % 2) + (z + j) % 4, 0, False)
        wa.append(split_shift(piece, j))
    w_own = lax.dynamic_index_in_dim(w_rows, 4 * xh + z, 0, False)
    ints = jnp.concatenate([block_mask.reshape(96), offsets, jnp.zeros((31,), jnp.int32)])
    rows = jnp.concatenate([lse, delta], axis=2).reshape(NL, 3, HD, 2, 3)
    small = jnp.transpose(rows, (1, 3, 0, 4, 2)).reshape(3, 2 * NLH, HD)
    xa, xb = split_tokens(co1, x_kv)
    xb = swap(xb)
    dkv, dqo, dqp = attn(
        ints, swap(ints), co1, vm(small), vm(swap(small)),
        vm(kv_all.reshape(KB, HD, 2 * HD)), queries, swap(queries), d_out, swap(d_out),
    )
    dkv_r = exchange(dkv.reshape(8, 256, 256), C8)
    (g,) = call(sum_kernel, [VM], ((256, 256), bf))(vm(dkv_r))
    dw_part, pair = weight_parts(co1, vm(xa), vm(xb), g, vm(swap(g)))
    dw_r = exchange(dw_part, C8)
    grad, sq = call(grad_kernel, [VM], ((192, 256), f32), ((128, HD), f32))(vm(dw_r))
    parts = exchange(sq.reshape(128, 1, HD), ALL)
    ra = [split_shift(pair, j) for j in range(4)]
    rb = [swap(r) for r in ra]
    wb = [swap(w) for w in wa]
    d_x = input_grads(co1, g, ra, rb, wb, wa, w_own)
    (d_queries,) = call(dq_kernel, [VM] * 2, ((NL, 384, 384), bf), near=False)(dqo, vm(swap(dqp)))
    (d_w,) = call(scale_kernel, [VM] * 2, ((192, 256), f32), near=False)(vm(grad), vm(parts.reshape(128, HD)))
    return (d_queries, d_x, d_w)


def solution(mesh):
    mesh5 = Mesh(mesh.devices.reshape(2, 4, 2, 2, 4), ALL)
    ctx = ("xl", "y", "co")
    kvh = ("xh", "z")
    in_specs = (
        P(ctx, None),
        P(None, kvh),
        P(None, ctx, kvh),
        P(None, ctx, kvh),
        P(None, ctx, kvh),
        P(None, ctx, kvh),
        P(ctx),
        P(ctx, None),
    )
    out_specs = (P(None, ctx, kvh), P(ctx, kvh), P(ctx, kvh))
    return jax.shard_map(step, mesh=mesh5, in_specs=in_specs, out_specs=out_specs, check_vma=False)
```
